128 devices in a mesh: row: 8 (over x, z_hi), col: 16 (over y, z_lo, core).
Axes of the slice: x: 4, y: 4, z: 4 (z_hi: 2, z_lo: 2; z = z_hi * 2 + z_lo), core: 2. Of those that a mesh axis runs over, the one named last changes fastest.
Arguments:
- panel_right: bfloat16 [128, 1536, 128], P('row', 'col'), may hold values from -1 to 1
- factor_inverse: bfloat16 [1536, 1536], replicated, as said below
- ranks: int32 [128], P(('row', 'col')), may hold values from 32 to 128
- owner_map: int32 [128], replicated, may hold values from 0 to 127, each once
- cores: float32 [8, 16, 16, 8, 128, 128], P('row', 'col'), may hold values from -6 to 6
Outputs:
- new_cores: float32 [8, 16, 16, 8, 128, 128], P('row', 'col')
The draws below stay inside these ranges and needn't reach their ends.
Inputs may be any that keep to these rules, and one draw needn't show every extreme that they name: `factor_inverse`: lower triangular, the inverse of a Cholesky factor.
All inputs are finite; a program needn't handle non-finite values.
Results may differ from the reference program's by a relative error of at most 0.0033.
Values may be sent and summed in bfloat16 or wider, within the bound.
A program may use at most 128 MiB of HBM per device.

```python
import jax
import jax.numpy as jnp
from jax import lax

B = 1536
R = 128
NP = 128
N_ROW = 8
N_COL = 16


def draw_factor_inverse(key, part):
    first, second = jax.random.split(key)
    spread = jax.random.normal(first, (B, B), jnp.float32)
    lower = jnp.tril(spread * (0.5 / B ** 0.5), -1)
    diagonal = jax.random.uniform(second, (B,), jnp.float32, 1.0, 2.0)
    return (lower + jnp.diag(diagonal)).astype(jnp.bfloat16)


def touch_ends(drawn, stream_key, least, largest):
    longest = drawn.shape.index(max(drawn.shape))
    spots = []
    for shift in (0, 1):
        where = [jax.random.randint(jax.random.fold_in(stream_key, axis), (), 0, length) for axis, length in enumerate(drawn.shape)]
        where[longest] = (where[longest] + shift) % drawn.shape[longest]
        spots.append(tuple(where))
    return drawn.at[spots[0]].set(least).at[spots[1]].set(largest)


def block_scale(stream_key, extent, cuts, smallest, top_value):
    factor_of = 1.0
    for position, blocks in cuts:
        draws = jax.random.uniform(jax.random.fold_in(jax.random.fold_in(stream_key, 6), position), (blocks,), jnp.float32, smallest / len(cuts), top_value / len(cuts))
        factor_of = factor_of * jnp.repeat(jnp.exp(draws), extent[position] // blocks).reshape((-1,) + (1,) * (len(extent) - 1 - position))
    return factor_of


def scatter_about(rng, extent, scale, most, cuts=(), kind=jnp.bfloat16):
    entries = jax.random.normal(rng, extent, jnp.float32) * scale
    if len(cuts) > 0:
        entries = block_scale(rng, extent, cuts, -0.22, 0.18) * entries
    return jnp.clip(entries, min=-most, max=most).astype(kind)


def setup_inputs(seed: int = 0) -> dict:
    splits = jax.random.split(jax.random.key(seed), 6)
    return {
        "panel_right": scatter_about(splits[0], (NP, B, R), 0.16, 1.0, ((0, 8), (1, 16))),
        "factor_inverse": draw_factor_inverse(jax.random.fold_in(splits[5], 71), 0),
        "ranks": touch_ends(jax.random.randint(splits[2], (NP,), R // 4, R + 1), jax.random.fold_in(splits[2], 1), R // 4, R).astype(jnp.int32),
        "owner_map": jax.random.permutation(splits[3], NP).astype(jnp.int32),
        "cores": scatter_about(splits[4], (N_ROW, N_COL, N_COL, N_ROW, R, R), 1.0, 6.0, ((0, 8), (1, 16)), jnp.float32),
    }


def reference(panel_right, factor_inverse, ranks, owner_map, cores):
    solved = jnp.einsum("ij,pjk->pik", factor_inverse.astype(jnp.float32), panel_right.astype(jnp.float32))
    column = lax.broadcasted_iota(jnp.int32, (1, 1, R), 2)
    keep = column < ranks.reshape(NP, 1, 1)
    panel_left = jnp.where(keep, solved, 0.0).astype(jnp.bfloat16)
    grid_map = owner_map.reshape(N_ROW, N_COL)
    right_side = panel_left[grid_map.reshape(NP)].reshape(N_ROW, N_COL, B, R).astype(jnp.float32)

    def one_row(row_index):
        lefts = panel_left[grid_map[row_index]].astype(jnp.float32)
        gram = jnp.einsum("aik,bcil->cabkl", lefts, right_side)
        return cores[row_index] - gram

    return lax.map(one_row, jnp.arange(N_ROW, dtype=jnp.int32))
```

```python
import jax
import jax.numpy as jnp
from jax import lax
from jax.experimental import pallas as pl
from jax.experimental.pallas import tpu as pltpu
from jax.sharding import PartitionSpec as P

B = 1536
R = 128
NP = 128
N_ROW = 8
N_COL = 16
ROWS = B // N_COL
PART = 16
PARTS = ROWS // PART
HB = B // 2
HR = R // 2
MESH = pl.DeviceIdType.MESH


def kernel(owner_ref, rank_ref, panel_hbm, inverse_hbm, cores_hbm, out_ref,
           spread, moved, held_rows, held, inverse, rank_mine, rank_rows, rank_pack, rank_all,
           right, left, send_sem, local_sem, sem_spread, sem_rank_a, sem_rank_b, sem_back, sem_rows,
           sem_right, sem_left):
    r = lax.axis_index("row")
    c = lax.axis_index("col")
    x, zh = r // 2, r % 2
    y, zl, h = c // 4, (c // 2) % 2, c % 2

    inverse_copy = pltpu.make_async_copy(inverse_hbm, inverse, local_sem.at[0])
    inverse_copy.start()
    cores_copy = pltpu.make_async_copy(cores_hbm, out_ref, local_sem.at[1])
    cores_copy.start()

    barrier = pltpu.get_barrier_semaphore()
    for d in range(1, N_ROW):
        pl.semaphore_signal(barrier, inc=1, device_id={"row": (r + d) % N_ROW, "col": c}, device_id_type=MESH)
    for d in range(1, N_COL):
        pl.semaphore_signal(barrier, inc=1, device_id={"row": r, "col": (c + d) % N_COL}, device_id_type=MESH)
    pl.semaphore_wait(barrier, N_ROW + N_COL - 2)

    sends = []
    counter = [0]

    def send(src, dst, recv, row, col, when=None):
        desc = pltpu.make_async_remote_copy(
            src_ref=src, dst_ref=dst, send_sem=send_sem.at[counter[0]], recv_sem=recv,
            device_id={"row": row, "col": col}, device_id_type=MESH)
        counter[0] += 1
        if when is None:
            desc.start()
        else:
            pl.when(when)(desc.start)
        sends.append((desc, when))

    def arrived(dst, recv):
        pltpu.make_async_remote_copy(
            src_ref=dst, dst_ref=dst, send_sem=recv, recv_sem=recv,
            device_id={"row": r, "col": c}, device_id_type=MESH).wait_recv()

    my_part = (r - c - 1) % N_ROW
    active = my_part < PARTS
    for d in range(1, N_ROW):
        to = (r + d) % N_ROW
        part = (to - c - 1) % N_ROW
        send(panel_hbm.at[:, pl.ds(pl.multiple_of(jnp.minimum(part, PARTS - 1) * PART, PART), PART), :],
             spread.at[pl.ds(r * N_COL, N_COL)], sem_spread.at[r], to, c, part < PARTS)
    own_part = pl.ds(pl.multiple_of(jnp.minimum(my_part, PARTS - 1) * PART, PART), PART)
    own_spread = pltpu.make_async_copy(
        panel_hbm.at[:, own_part, :], spread.at[pl.ds(r * N_COL, N_COL)], local_sem.at[2])
    pl.when(active)(own_spread.start)

    rank_mine[...] = jnp.full((8, R), rank_ref[0], jnp.int32)
    for d in range(1, N_ROW):
        send(rank_mine, rank_rows.at[r], sem_rank_a.at[r], (r + d) % N_ROW, c)
    rank_rows[r] = rank_mine[...]

    @pl.when(active)
    def _():
        own_spread.wait()
        for d in range(1, N_ROW):
            frm = (r + d) % N_ROW
            arrived(spread.at[pl.ds(frm * N_COL, N_COL)], sem_spread.at[frm])

        @pl.loop(0, NP, unroll=8)
        def _(p):
            moved[p] = spread[owner_ref[p]]

    for d in range(1, N_ROW):
        to = (r + d) % N_ROW
        send(moved.at[pl.ds(to * N_COL, N_COL)], held_rows.at[:, own_part, :],
             sem_back.at[my_part], to, c, active)
    own_back = pltpu.make_async_copy(
        moved.at[pl.ds(r * N_COL, N_COL)], held_rows.at[:, own_part, :], local_sem.at[2])
    pl.when(active)(own_back.start)

    for d in range(1, N_ROW):
        frm = (r + d) % N_ROW
        arrived(rank_rows.at[frm], sem_rank_a.at[frm])
    for k in range(N_ROW):
        rank_pack[pl.ds(k, 1), :] = rank_rows[k, pl.ds(0, 1), :]
    for d in range(1, N_COL):
        send(rank_pack, rank_all.at[c], sem_rank_b.at[c], r, (c + d) % N_COL)
    rank_all[c] = rank_pack[...]

    pl.when(active)(own_back.wait)
    for part in range(PARTS):
        frm = (part + c + 1) % N_ROW

        @pl.when(frm != r)
        def _(part=part):
            arrived(held_rows.at[:, pl.ds(part * PART, PART), :], sem_back.at[part])

    for d in range(1, N_COL):
        to = (c + d) % N_COL
        send(held_rows.at[to], held.at[pl.ds(pl.multiple_of(c * ROWS, 16), ROWS), :], sem_rows.at[c], r, to)
    own_rows = pltpu.make_async_copy(
        held_rows.at[c], held.at[pl.ds(pl.multiple_of(c * ROWS, 16), ROWS), :], local_sem.at[2])
    own_rows.start()
    for d in range(1, N_COL):
        frm = (c + d) % N_COL
        arrived(rank_all.at[frm], sem_rank_b.at[frm])
    inverse_copy.wait()
    own_rows.wait()
    for d in range(1, N_COL):
        frm = (c + d) % N_COL
        arrived(held.at[pl.ds(pl.multiple_of(frm * ROWS, 16), ROWS), :], sem_rows.at[frm])

    block = owner_ref[r * N_COL + c]
    rank = rank_all[block % N_COL, pl.ds(block // N_COL, 1), :]
    keep = lax.broadcasted_iota(jnp.int32, (1, R), 1) < rank
    step = 256
    for i in range(B // step):
        rows = slice(i * step, (i + 1) * step)
        done = (i + 1) * step
        solved = jnp.dot(inverse[rows, :done], held[:done, :], preferred_element_type=jnp.float32)
        solved = jnp.where(keep, solved, 0.0)
        right[r, rows, :] = solved.astype(jnp.bfloat16)
        left[c, :, rows] = solved.T.astype(jnp.bfloat16)

    def row_of(dx, flip):
        return ((x + dx) % 4) * 2 + (1 - zh if flip else zh)

    def col_of(dy, flip, other=0):
        return ((y + dy) % 4) * 4 + (1 - zl if flip else zl) * 2 + (1 - h if other else h)

    sibling = col_of(0, 0, 1)

    def send_right(slot, dx, flip, part=None):
        if part is None:
            ref, sem = right.at[slot], sem_right.at[slot, 0]
        else:
            ref, sem = right.at[slot, pl.ds(part * HB, HB), :], sem_right.at[slot, part]
        send(ref, ref, sem, row_of(dx, flip), c)

    def send_left(slot, to, part=None):
        if part is None:
            ref, sem = left.at[slot], sem_left.at[slot, 0]
        else:
            ref, sem = left.at[slot, pl.ds(part * HR, HR), :], sem_left.at[slot, part]
        send(ref, ref, sem, r, to)

    def wait_right(slot):
        arrived(right.at[slot], sem_right.at[slot, 0])

    def wait_left(slot):
        arrived(left.at[slot], sem_left.at[slot, 0])

    def wait_halves(ref, sem, slot, half):
        for part in range(2):
            arrived(ref.at[slot, pl.ds(part * half, half), :], sem.at[slot, part])

    def gram(pairs, first, second):
        for pair in pairs:
            lhs = left[pl.ds(pair * 2, 2)].reshape(2 * R, B)
            rhs = jnp.concatenate([right[first], right[second]], axis=1)
            g = jnp.dot(lhs, rhs, preferred_element_type=jnp.float32)
            for i in range(2):
                for j, slot in enumerate((first, second)):
                    out_ref[pair * 2 + i, slot] -= g[i * R:(i + 1) * R, j * R:(j + 1) * R]

    def pair_of(dy, flip):
        return ((y + dy) % 4) * 2 + (1 - zl if flip else zl)

    def gram_set(pairs, rights):
        for first, second in rights:
            gram(pairs, first, second)

    own_pair = (row_of(0, 0), row_of(0, 1))
    near_o = (row_of(-1, 0), row_of(1, 0))
    near_q = (row_of(-1, 1), row_of(1, 1))
    far = (row_of(2, 0), row_of(2, 1))

    for dx in (1, -1):
        send_right(r, dx, 0)
    send_right(r, 0, 1)
    for dy in (1, -1):
        send_left(c, col_of(dy, 0))
    send_left(c, col_of(0, 1))
    send_left(c, sibling)

    wait_right(row_of(0, 1))
    for dx in (1, -1):
        send_right(row_of(0, 1), dx, 0)
    wait_left(col_of(0, 1))
    for dy in (1, -1):
        send_left(col_of(0, 1), col_of(dy, 0))
    send_left(col_of(0, 1), sibling)

    cores_copy.wait()
    wait_left(col_of(0, 0, 1))
    gram_set([pair_of(0, 0)], [own_pair])

    for part, d in ((0, -1), (1, 1)):
        wait_right(row_of(d, 0))
        send_right(row_of(d, 0), -d, 0, part)
    for part, d in ((0, -1), (1, 1)):
        wait_left(col_of(d, 0))
        send_left(col_of(d, 0), col_of(-d, 0), part)
        send_left(col_of(d, 0), sibling)

    wait_left(col_of(0, 1, 1))
    gram_set([pair_of(0, 0)], [near_o])
    gram_set([pair_of(0, 1)], [own_pair, near_o])
    wait_halves(right, sem_right, row_of(2, 0), HB)
    wait_halves(left, sem_left, col_of(2, 0), HR)
    send_left(col_of(2, 0), sibling)
    for d in (-1, 1):
        wait_left(col_of(d, 0, 1))
        gram_set([pair_of(d, 0)], [own_pair, near_o])

    for part, d in ((0, -1), (1, 1)):
        wait_right(row_of(d, 1))
        send_right(row_of(d, 1), -d, 0, part)
    for part, d in ((0, -1), (1, 1)):
        wait_left(col_of(d, 1))
        send_left(col_of(d, 1), col_of(-d, 0), part)
        send_left(col_of(d, 1), sibling)
    wait_left(col_of(2, 0, 1))
    gram_set([pair_of(2, 0)], [own_pair, near_o, near_q])
    gram_set([pair_of(0, 0), pair_of(0, 1), pair_of(-1, 0), pair_of(1, 0)], [near_q])
    for d in (-1, 1):
        wait_left(col_of(d, 1, 1))
        gram_set([pair_of(d, 1)], [own_pair, near_o, near_q])

    wait_halves(left, sem_left, col_of(2, 1), HR)
    send_left(col_of(2, 1), sibling)
    wait_halves(right, sem_right, row_of(2, 1), HB)
    gram_set([pair_of(0, 0), pair_of(0, 1), pair_of(-1, 0), pair_of(1, 0), pair_of(2, 0),
              pair_of(-1, 1), pair_of(1, 1)], [far])
    wait_left(col_of(2, 1, 1))
    gram_set([pair_of(2, 1)], [own_pair, near_o, near_q, far])

    for desc, when in sends:
        if when is None:
            desc.wait_send()
        else:
            pl.when(when)(desc.wait_send)


def body(panel_right, factor_inverse, ranks, owner_map, cores):
    grams = 16 * 8 * 128 * 128
    vmem = pl.BlockSpec(memory_space=pltpu.VMEM)
    smem = pl.BlockSpec(memory_space=pltpu.SMEM)
    anywhere = pl.BlockSpec(memory_space=pl.ANY)
    bf16 = jnp.bfloat16
    dma = pltpu.SemaphoreType.DMA
    out = pl.pallas_call(
        kernel,
        out_shape=jax.ShapeDtypeStruct((N_COL, N_ROW, R, R), jnp.float32),
        in_specs=[smem, smem, anywhere, anywhere, anywhere],
        out_specs=vmem,
        scratch_shapes=[
            pltpu.VMEM((NP, PART, R), bf16),
            pltpu.VMEM((NP, PART, R), bf16),
            pltpu.VMEM((N_COL, ROWS, R), bf16),
            pltpu.VMEM((B, R), bf16),
            pltpu.VMEM((B, B), bf16),
            pltpu.VMEM((8, R), jnp.int32),
            pltpu.VMEM((N_ROW, 8, R), jnp.int32),
            pltpu.VMEM((8, R), jnp.int32),
            pltpu.VMEM((N_COL, 8, R), jnp.int32),
            pltpu.VMEM((N_ROW, B, R), bf16),
            pltpu.VMEM((N_COL, R, B), bf16),
            dma((96,)),
            dma((3,)),
            dma((N_ROW,)),
            dma((N_ROW,)),
            dma((N_COL,)),
            dma((N_ROW,)),
            dma((N_COL,)),
            dma((N_ROW, 2)),
            dma((N_COL, 2)),
        ],
        compiler_params=pltpu.CompilerParams(
            collective_id=0, has_side_effects=True, vmem_limit_bytes=48 << 20),
        cost_estimate=pl.CostEstimate(
            flops=2 * grams * B, bytes_accessed=4 * grams * 2, transcendentals=0),
    )(owner_map, ranks, panel_right, factor_inverse, cores.reshape(N_COL, N_ROW, R, R))
    return out.reshape(cores.shape)


def solution(mesh):
    return jax.shard_map(
        body,
        mesh=mesh,
        in_specs=(
            P("row", "col", None),
            P(),
            P(("row", "col")),
            P(),
            P("row", "col", None, None, None, None),
        ),
        out_specs=P("row", "col", None, None, None, None),
        check_vma=False,
    )
```

```python
import jax
import jax.numpy as jnp
from jax import lax
from jax.experimental import pallas as pl
from jax.experimental.pallas import tpu as pltpu
from jax.sharding import PartitionSpec as P

B = 1536
R = 128
NP = 128
N_ROW = 8
N_COL = 16
ROWS = B // N_COL
PART = 16
PARTS = ROWS // PART
HB = B // 2
HR = R // 2
MESH = pl.DeviceIdType.MESH


def kernel(owner_ref, rank_ref, panel_hbm, inverse_hbm, cores_hbm, out_ref,
           spread, moved, held_rows, held, inverse, rank_mine, rank_rows, rank_pack, rank_all,
           right, left, send_sem, local_sem, sem_spread, sem_rank_a, sem_rank_b, sem_back, sem_rows,
           sem_right, sem_left):
    r = lax.axis_index("row")
    c = lax.axis_index("col")
    x, zh = r // 2, r % 2
    y, zl, h = c // 4, (c // 2) % 2, c % 2

    inverse_copy = pltpu.make_async_copy(inverse_hbm, inverse, local_sem.at[0])
    inverse_copy.start()
    cores_copy = pltpu.make_async_copy(cores_hbm, out_ref, local_sem.at[1])
    cores_copy.start()

    barrier = pltpu.get_barrier_semaphore()
    for d in range(1, N_ROW):
        pl.semaphore_signal(barrier, inc=1, device_id={"row": (r + d) % N_ROW, "col": c}, device_id_type=MESH)
    for d in range(1, N_COL):
        pl.semaphore_signal(barrier, inc=1, device_id={"row": r, "col": (c + d) % N_COL}, device_id_type=MESH)
    pl.semaphore_wait(barrier, N_ROW + N_COL - 2)

    sends = []
    counter = [0]

    def send(src, dst, recv, row, col, when=None):
        desc = pltpu.make_async_remote_copy(
            src_ref=src, dst_ref=dst, send_sem=send_sem.at[counter[0]], recv_sem=recv,
            device_id={"row": row, "col": col}, device_id_type=MESH)
        counter[0] += 1
        if when is None:
            desc.start()
        else:
            pl.when(when)(desc.start)
        sends.append((desc, when))

    def arrived(dst, recv):
        pltpu.make_async_remote_copy(
            src_ref=dst, dst_ref=dst, send_sem=recv, recv_sem=recv,
            device_id={"row": r, "col": c}, device_id_type=MESH).wait_recv()

    my_part = (r - c - 1) % N_ROW
    active = my_part < PARTS
    for d in range(1, N_ROW):
        to = (r + d) % N_ROW
        part = (to - c - 1) % N_ROW
        send(panel_hbm.at[:, pl.ds(pl.multiple_of(jnp.minimum(part, PARTS - 1) * PART, PART), PART), :],
             spread.at[pl.ds(r * N_COL, N_COL)], sem_spread.at[r], to, c, part < PARTS)
    own_part = pl.ds(pl.multiple_of(jnp.minimum(my_part, PARTS - 1) * PART, PART), PART)
    own_spread = pltpu.make_async_copy(
        panel_hbm.at[:, own_part, :], spread.at[pl.ds(r * N_COL, N_COL)], local_sem.at[2])
    pl.when(active)(own_spread.start)

    rank_mine[...] = jnp.full((8, R), rank_ref[0], jnp.int32)
    for d in range(1, N_ROW):
        send(rank_mine, rank_rows.at[r], sem_rank_a.at[r], (r + d) % N_ROW, c)
    rank_rows[r] = rank_mine[...]

    @pl.when(active)
    def _():
        own_spread.wait()
        for d in range(1, N_ROW):
            frm = (r + d) % N_ROW
            arrived(spread.at[pl.ds(frm * N_COL, N_COL)], sem_spread.at[frm])

        @pl.loop(0, NP, unroll=8)
        def _(p):
            moved[p] = spread[owner_ref[p]]

    for d in range(1, N_ROW):
        to = (r + d) % N_ROW
        send(moved.at[pl.ds(to * N_COL, N_COL)], held_rows.at[:, own_part, :],
             sem_back.at[my_part], to, c, active)
    own_back = pltpu.make_async_copy(
        moved.at[pl.ds(r * N_COL, N_COL)], held_rows.at[:, own_part, :], local_sem.at[2])
    pl.when(active)(own_back.start)

    for d in range(1, N_ROW):
        frm = (r + d) % N_ROW
        arrived(rank_rows.at[frm], sem_rank_a.at[frm])
    for k in range(N_ROW):
        rank_pack[pl.ds(k, 1), :] = rank_rows[k, pl.ds(0, 1), :]
    for d in range(1, N_COL):
        send(rank_pack, rank_all.at[c], sem_rank_b.at[c], r, (c + d) % N_COL)
    rank_all[c] = rank_pack[...]

    pl.when(active)(own_back.wait)
    for part in range(PARTS):
        frm = (part + c + 1) % N_ROW

        @pl.when(frm != r)
        def _(part=part):
            arrived(held_rows.at[:, pl.ds(part * PART, PART), :], sem_back.at[part])

    for d in range(1, N_COL):
        to = (c + d) % N_COL
        send(held_rows.at[to], held.at[pl.ds(pl.multiple_of(c * ROWS, 16), ROWS), :], sem_rows.at[c], r, to)
    own_rows = pltpu.make_async_copy(
        held_rows.at[c], held.at[pl.ds(pl.multiple_of(c * ROWS, 16), ROWS), :], local_sem.at[2])
    own_rows.start()
    for d in range(1, N_COL):
        frm = (c + d) % N_COL
        arrived(rank_all.at[frm], sem_rank_b.at[frm])
    inverse_copy.wait()
    own_rows.wait()
    for d in range(1, N_COL):
        frm = (c + d) % N_COL
        arrived(held.at[pl.ds(pl.multiple_of(frm * ROWS, 16), ROWS), :], sem_rows.at[frm])

    block = owner_ref[r * N_COL + c]
    rank = rank_all[block % N_COL, pl.ds(block // N_COL, 1), :]
    keep = lax.broadcasted_iota(jnp.int32, (1, R), 1) < rank
    step = 256
    for i in range(B // step):
        rows = slice(i * step, (i + 1) * step)
        done = (i + 1) * step
        solved = jnp.dot(inverse[rows, :done], held[:done, :], preferred_element_type=jnp.float32)
        solved = jnp.where(keep, solved, 0.0)
        right[r, rows, :] = solved.astype(jnp.bfloat16)
        left[c, :, rows] = solved.T.astype(jnp.bfloat16)

    def row_of(dx, flip):
        return ((x + dx) % 4) * 2 + (1 - zh if flip else zh)

    def col_of(dy, flip, other=0):
        return ((y + dy) % 4) * 4 + (1 - zl if flip else zl) * 2 + (1 - h if other else h)

    sibling = col_of(0, 0, 1)

    def half(ref, slot, part):
        size = HB if ref is right else HR
        return ref.at[slot, pl.ds(part * size, size), :]

    def send_right(slot, part, dx, flip=0):
        ref = half(right, slot, part)
        send(ref, ref, sem_right.at[slot, part], row_of(dx, flip), c)

    def send_left(slot, part, dy, flip=0):
        ref = half(left, slot, part)
        send(ref, ref, sem_left.at[slot, part], r, col_of(dy, flip))

    def share(slot):
        send(left.at[slot], left.at[slot], sem_left.at[slot, 0], r, sibling)

    def wait_right(slot, part):
        arrived(half(right, slot, part), sem_right.at[slot, part])

    def wait_left(slot, part):
        arrived(half(left, slot, part), sem_left.at[slot, part])

    def wait_shared(slot):
        arrived(left.at[slot], sem_left.at[slot, 0])

    def gram(pair, first, second):
        lhs = left[pl.ds(pair * 2, 2)].reshape(2 * R, B)
        rhs = jnp.concatenate([right[first], right[second]], axis=1)
        g = jnp.dot(lhs, rhs, preferred_element_type=jnp.float32)
        for i in range(2):
            for j, slot in enumerate((first, second)):
                out_ref[pair * 2 + i, slot] -= g[i * R:(i + 1) * R, j * R:(j + 1) * R]

    def pair_of(dy, flip):
        return ((y + dy) % 4) * 2 + (1 - zl if flip else zl)

    near_o = (row_of(-1, 0), row_of(1, 0))
    own_far = (row_of(0, 0), row_of(2, 0))
    near_q = (row_of(-1, 1), row_of(1, 1))
    flip_far = (row_of(0, 1), row_of(2, 1))
    r_q, c_q = row_of(0, 1), col_of(0, 1)
    toward = ((0, 1), (1, -1))

    send_left(c, 0, 0, 1)
    send_right(r, 0, 0, 1)
    for part, d in toward:
        send_right(r, part, d)
        send_left(c, part, d)
    for part, d in toward:
        send_right(r, 1 - part, d)
        send_left(c, 1 - part, d)
    send_left(c, 1, 0, 1)
    send_right(r, 1, 0, 1)
    share(c)

    for part, d in toward:
        wait_right(row_of(-d, 0), part)
        send_right(row_of(-d, 0), part, d)
        wait_left(col_of(-d, 0), part)
        send_left(col_of(-d, 0), part, d)
    wait_left(c_q, 0)
    for d in (1, -1):
        send_left(c_q, 0, d)
    wait_right(r_q, 0)
    for d in (1, -1):
        send_right(r_q, 0, d)
    cores_copy.wait()
    wait_shared(col_of(0, 0, 1))

    for part, d in toward:
        wait_right(row_of(-d, 0), 1 - part)
        wait_left(col_of(-d, 0), 1 - part)
        share(col_of(-d, 0))
    gram(pair_of(0, 0), *near_o)

    wait_left(c_q, 1)
    for d in (1, -1):
        send_left(c_q, 1, d)
    share(c_q)
    for part in range(2):
        wait_right(row_of(2, 0), part)
        wait_left(col_of(2, 0), part)
    share(col_of(2, 0))
    for d in (-1, 1):
        wait_shared(col_of(d, 0, 1))
        gram(pair_of(d, 0), *near_o)
    wait_right(r_q, 1)
    for d in (1, -1):
        send_right(r_q, 1, d)

    wait_shared(col_of(0, 1, 1))
    gram(pair_of(0, 1), *near_o)
    gram(pair_of(0, 1), *own_far)
    gram(pair_of(0, 0), *own_far)
    for part, d in toward:
        wait_left(col_of(-d, 1), part)
        send_left(col_of(-d, 1), part, d)
    wait_shared(col_of(2, 0, 1))
    gram(pair_of(2, 0), *near_o)
    gram(pair_of(2, 0), *own_far)
    for part, d in toward:
        wait_right(row_of(-d, 1), part)
        send_right(row_of(-d, 1), part, d)
    for d in (-1, 1):
        gram(pair_of(d, 0), *own_far)
    for part, d in toward:
        wait_left(col_of(-d, 1), 1 - part)
        share(col_of(-d, 1))
    for d in (-1, 1):
        wait_shared(col_of(d, 1, 1))
        gram(pair_of(d, 1), *near_o)
        gram(pair_of(d, 1), *own_far)
    for part, d in toward:
        wait_right(row_of(-d, 1), 1 - part)
    for pair in (pair_of(0, 0), pair_of(0, 1), pair_of(2, 0), pair_of(-1, 0), pair_of(1, 0), pair_of(-1, 1), pair_of(1, 1)):
        gram(pair, *near_q)

    for part in range(2):
        wait_left(col_of(2, 1), part)
    share(col_of(2, 1))
    for part in range(2):
        wait_right(row_of(2, 1), part)
    for pair in (pair_of(0, 0), pair_of(0, 1), pair_of(2, 0), pair_of(-1, 0), pair_of(1, 0), pair_of(-1, 1), pair_of(1, 1)):
        gram(pair, *flip_far)
    wait_shared(col_of(2, 1, 1))
    for rights in (near_o, own_far, near_q, flip_far):
        gram(pair_of(2, 1), *rights)

    for desc, when in sends:
        if when is None:
            desc.wait_send()
        else:
            pl.when(when)(desc.wait_send)


def body(panel_right, factor_inverse, ranks, owner_map, cores):
    grams = 16 * 8 * 128 * 128
    vmem = pl.BlockSpec(memory_space=pltpu.VMEM)
    smem = pl.BlockSpec(memory_space=pltpu.SMEM)
    hbm = pl.BlockSpec(memory_space=pltpu.HBM)
    bf16 = jnp.bfloat16
    dma = pltpu.SemaphoreType.DMA
    out = pl.pallas_call(
        kernel,
        out_shape=pltpu.VMEM((N_COL, N_ROW, R, R), jnp.float32),
        in_specs=[smem, smem, hbm, hbm, hbm],
        out_specs=vmem,
        scratch_shapes=[
            pltpu.VMEM((NP, PART, R), bf16),
            pltpu.VMEM((NP, PART, R), bf16),
            pltpu.VMEM((N_COL, ROWS, R), bf16),
            pltpu.VMEM((B, R), bf16),
            pltpu.VMEM((B, B), bf16),
            pltpu.VMEM((8, R), jnp.int32),
            pltpu.VMEM((N_ROW, 8, R), jnp.int32),
            pltpu.VMEM((8, R), jnp.int32),
            pltpu.VMEM((N_COL, 8, R), jnp.int32),
            pltpu.VMEM((N_ROW, B, R), bf16),
            pltpu.VMEM((N_COL, R, B), bf16),
            dma((96,)),
            dma((3,)),
            dma((N_ROW,)),
            dma((N_ROW,)),
            dma((N_COL,)),
            dma((N_ROW,)),
            dma((N_COL,)),
            dma((N_ROW, 2)),
            dma((N_COL, 2)),
        ],
        compiler_params=pltpu.CompilerParams(
            collective_id=0, has_side_effects=True, vmem_limit_bytes=48 << 20),
        cost_estimate=pl.CostEstimate(
            flops=2 * grams * B, bytes_accessed=4 * grams * 2, transcendentals=0),
    )(owner_map, ranks, panel_right, factor_inverse, cores.reshape(N_COL, N_ROW, R, R))
    return out.reshape(cores.shape)


def solution(mesh):
    return jax.shard_map(
        body,
        mesh=mesh,
        in_specs=(
            P("row", "col", None),
            P(),
            P(("row", "col")),
            P(),
            P("row", "col", None, None, None, None),
        ),
        out_specs=P("row", "col", None, None, None, None),
        check_vma=False,
    )
```

```python
import jax
import jax.numpy as jnp
from jax import lax
from jax.experimental import pallas as pl
from jax.experimental.pallas import tpu as pltpu
from jax.sharding import PartitionSpec as P

B = 1536
R = 128
NP = 128
N_ROW = 8
N_COL = 16
ROWS = B // N_COL
PART = 16
PARTS = ROWS // PART
CUTS = 4
MESH = pl.DeviceIdType.MESH


def kernel(owner_ref, rank_ref, panel_hbm, inverse_hbm, cores_hbm, out_ref,
           spread, moved, held, inverse, rank_mine, rank_rows, rank_pack, rank_all,
           right, left, send_sem, local_sem, sem_spread, sem_rank_a, sem_rank_b, sem_moved, sem_rows,
           sem_right, sem_left):
    r = lax.axis_index("row")
    c = lax.axis_index("col")
    x, zh = r // 2, r % 2
    y, zl, h = c // 4, (c // 2) % 2, c % 2

    inverse_copy = pltpu.make_async_copy(inverse_hbm, inverse, local_sem.at[0])
    inverse_copy.start()
    cores_copy = pltpu.make_async_copy(cores_hbm, out_ref, local_sem.at[1])
    cores_copy.start()

    barrier = pltpu.get_barrier_semaphore()
    for d in range(1, N_ROW):
        pl.semaphore_signal(barrier, inc=1, device_id={"row": (r + d) % N_ROW, "col": c}, device_id_type=MESH)
    for d in range(1, N_COL):
        pl.semaphore_signal(barrier, inc=1, device_id={"row": r, "col": (c + d) % N_COL}, device_id_type=MESH)
    pl.semaphore_wait(barrier, N_ROW + N_COL - 2)

    sends = []
    counter = [0]

    def send(src, dst, recv, row, col, when=None):
        desc = pltpu.make_async_remote_copy(
            src_ref=src, dst_ref=dst, send_sem=send_sem.at[counter[0]], recv_sem=recv,
            device_id={"row": row, "col": col}, device_id_type=MESH)
        counter[0] += 1
        if when is None:
            desc.start()
        else:
            pl.when(when)(desc.start)
        sends.append((desc, when))

    def arrived(dst, recv):
        pltpu.make_async_remote_copy(
            src_ref=dst, dst_ref=dst, send_sem=recv, recv_sem=recv,
            device_id={"row": r, "col": c}, device_id_type=MESH).wait_recv()

    my_part = (r - c - 1) % N_ROW
    active = my_part < PARTS
    for d in range(1, N_ROW):
        to = (r + d) % N_ROW
        part = (to - c - 1) % N_ROW
        send(panel_hbm.at[:, pl.ds(pl.multiple_of(jnp.minimum(part, PARTS - 1) * PART, PART), PART), :],
             spread.at[pl.ds(r * N_COL, N_COL)], sem_spread.at[r], to, c, part < PARTS)
    own_part = pl.ds(pl.multiple_of(jnp.minimum(my_part, PARTS - 1) * PART, PART), PART)
    own_spread = pltpu.make_async_copy(
        panel_hbm.at[:, own_part, :], spread.at[pl.ds(r * N_COL, N_COL)], local_sem.at[2])
    pl.when(active)(own_spread.start)

    rank_mine[...] = jnp.full((8, R), rank_ref[0], jnp.int32)
    for d in range(1, N_ROW):
        send(rank_mine, rank_rows.at[r], sem_rank_a.at[r], (r + d) % N_ROW, c)
    rank_rows[r] = rank_mine[...]

    @pl.when(active)
    def _():
        own_spread.wait()
        for d in range(1, N_ROW):
            frm = (r + d) % N_ROW
            arrived(spread.at[pl.ds(frm * N_COL, N_COL)], sem_spread.at[frm])

        @pl.loop(0, NP, unroll=8)
        def _(p):
            moved[p] = spread[owner_ref[p]]

    for d in range(1, N_ROW):
        frm = (r + d) % N_ROW
        arrived(rank_rows.at[frm], sem_rank_a.at[frm])
    me = r * N_COL + c
    own_rows = pl.ds(pl.multiple_of(c * ROWS + jnp.minimum(my_part, PARTS - 1) * PART, PART), PART)
    own_copy = pltpu.make_async_copy(moved.at[me], held.at[own_rows, :], local_sem.at[2])

    @pl.when(active)
    def _():
        @pl.loop(1, NP)
        def _(d):
            p = (me + d) % NP
            pltpu.make_async_remote_copy(
                src_ref=moved.at[p], dst_ref=held.at[own_rows, :],
                send_sem=sem_moved.at[0], recv_sem=sem_rows.at[0],
                device_id={"row": p // N_COL, "col": p % N_COL}, device_id_type=MESH).start()
        own_copy.start()

    for k in range(N_ROW):
        rank_pack[pl.ds(k, 1), :] = rank_rows[k, pl.ds(0, 1), :]
    for d in range(1, N_COL):
        send(rank_pack, rank_all.at[c], sem_rank_b.at[c], r, (c + d) % N_COL)
    rank_all[c] = rank_pack[...]
    for d in range(1, N_COL):
        frm = (c + d) % N_COL
        arrived(rank_all.at[frm], sem_rank_b.at[frm])
    inverse_copy.wait()

    @pl.when(active)
    def _():
        own_copy.wait()
        arrived(held.at[pl.ds(0, B - PART), :], sem_rows.at[0])

    @pl.when(jnp.logical_not(active))
    def _():
        arrived(held, sem_rows.at[0])

    block = owner_ref[r * N_COL + c]
    rank = rank_all[block % N_COL, pl.ds(block // N_COL, 1), :]
    keep = lax.broadcasted_iota(jnp.int32, (1, R), 1) < rank
    step = 256
    for i in range(B // step):
        rows = slice(i * step, (i + 1) * step)
        done = (i + 1) * step
        solved = jnp.dot(inverse[rows, :done], held[:done, :], preferred_element_type=jnp.float32)
        solved = jnp.where(keep, solved, 0.0)
        right[r, rows, :] = solved.astype(jnp.bfloat16)
        left[c, :, rows] = solved.T.astype(jnp.bfloat16)

    def row_of(dx, flip):
        return ((x + dx) % 4) * 2 + (1 - zh if flip else zh)

    def col_of(dy, flip, other=0):
        return ((y + dy) % 4) * 4 + (1 - zl if flip else zl) * 2 + (1 - h if other else h)

    sibling = col_of(0, 0, 1)

    def half(ref, slot, part):
        size = ref.shape[1] // CUTS
        return ref.at[slot, pl.ds(part * size, size), :]

    def send_right(slot, part, dx, flip=0):
        ref = half(right, slot, part)
        send(ref, ref, sem_right.at[slot, part], row_of(dx, flip), c)

    def send_left(slot, part, dy, flip=0):
        ref = half(left, slot, part)
        send(ref, ref, sem_left.at[slot, part], r, col_of(dy, flip))

    def share(slot):
        send(left.at[slot], left.at[slot], sem_left.at[slot, 0], r, sibling)

    def wait_right(slot, part):
        arrived(half(right, slot, part), sem_right.at[slot, part])

    def wait_left(slot, part):
        arrived(half(left, slot, part), sem_left.at[slot, part])

    def wait_shared(slot):
        arrived(left.at[slot], sem_left.at[slot, 0])

    def gram(pair, first, second):
        lhs = left[pl.ds(pair * 2, 2)].reshape(2 * R, B)
        rhs = jnp.concatenate([right[first], right[second]], axis=1)
        g = jnp.dot(lhs, rhs, preferred_element_type=jnp.float32)
        for i in range(2):
            for j, slot in enumerate((first, second)):
                out_ref[pair * 2 + i, slot] -= g[i * R:(i + 1) * R, j * R:(j + 1) * R]

    def pair_of(dy, flip):
        return ((y + dy) % 4) * 2 + (1 - zl if flip else zl)

    near_o = (row_of(-1, 0), row_of(1, 0))
    own_far = (row_of(0, 0), row_of(2, 0))
    near_q = (row_of(-1, 1), row_of(1, 1))
    flip_far = (row_of(0, 1), row_of(2, 1))
    r_q, c_q = row_of(0, 1), col_of(0, 1)
    toward = ((0, 1), (2, -1))
    order = (0, 2, 1, 3)

    def near_right(flip, part, d, on):
        wait_right(row_of(-d, flip), part)
        if on:
            send_right(row_of(-d, flip), part, d)

    def near_left(flip, part, d, on):
        wait_left(col_of(-d, flip), part)
        if on:
            send_left(col_of(-d, flip), part, d)

    def near(flip, step):
        for first, d in toward:
            part = (first + step) % CUTS
            near_right(flip, part, d, step < 2)
            near_left(flip, part, d, step < 2)

    def near_flip(part):
        for first, d in toward:
            on = part - first in (0, 1)
            near_right(1, part, d, on)
            near_left(1, part, d, on)

    def flip_left(part):
        wait_left(c_q, part)
        for d in (1, -1):
            send_left(c_q, part, d)

    def flip_right(part):
        wait_right(r_q, part)
        for d in (1, -1):
            send_right(r_q, part, d)

    def far(flip, step):
        for first, d in toward:
            wait_right(row_of(2, flip), first + step)
            wait_left(col_of(2, flip), first + step)

    def grams(pairs, *rights):
        for pair in pairs:
            for pick in rights:
                gram(pair, *pick)

    send_left(c, 0, 0, 1)
    send_right(r, 0, 0, 1)
    for step in range(CUTS):
        for first, d in toward:
            send_right(r, (first + step) % CUTS, d)
            send_left(c, (first + step) % CUTS, d)
        if step:
            send_left(c, order[step], 0, 1)
            send_right(r, order[step], 0, 1)
    share(c)
    here, here_q, away, away_q = pair_of(0, 0), pair_of(0, 1), pair_of(2, 0), pair_of(2, 1)
    beside = (pair_of(-1, 0), pair_of(1, 0))
    beside_q = (pair_of(-1, 1), pair_of(1, 1))

    near(0, 0)
    flip_left(0)
    near(0, 1)
    flip_right(0)
    cores_copy.wait()
    wait_shared(col_of(0, 0, 1))
    near(0, 2)
    flip_left(2)
    near(0, 3)
    flip_right(2)
    for d in (1, -1):
        share(col_of(d, 0))
    far(0, 0)
    flip_left(1)
    grams((here,), near_o)
    near_flip(0)
    flip_right(1)
    for d in (1, -1):
        wait_shared(col_of(d, 0, 1))
    grams(beside, near_o)
    far(0, 1)
    share(col_of(2, 0))
    flip_left(3)
    share(c_q)
    grams((here,), own_far)
    near_flip(2)
    flip_right(3)
    grams(beside, own_far)
    near_flip(1)
    wait_shared(col_of(2, 0, 1))
    grams((away,), near_o, own_far)
    wait_shared(col_of(0, 1, 1))
    near_flip(3)
    for d in (1, -1):
        share(col_of(d, 1))
    grams((here_q,), near_o, own_far)
    grams((here, here_q), near_q)
    far(1, 0)
    grams(beside + (away,), near_q)
    for d in (1, -1):
        wait_shared(col_of(d, 1, 1))
    far(1, 1)
    share(col_of(2, 1))
    grams(beside_q, near_o, own_far, near_q)
    grams((here, here_q, away) + beside + beside_q, flip_far)
    wait_shared(col_of(2, 1, 1))
    grams((away_q,), near_o, own_far, near_q, flip_far)

    @pl.when(active)
    def _():
        pltpu.make_async_remote_copy(
            src_ref=moved.at[pl.ds(0, NP - 1)], dst_ref=moved.at[pl.ds(0, NP - 1)],
            send_sem=sem_moved.at[0], recv_sem=sem_moved.at[0],
            device_id={"row": r, "col": c}, device_id_type=MESH).wait_send()

    for desc, when in sends:
        if when is None:
            desc.wait_send()
        else:
            pl.when(when)(desc.wait_send)


def body(panel_right, factor_inverse, ranks, owner_map, cores):
    grams = 16 * 8 * 128 * 128
    vmem = pl.BlockSpec(memory_space=pltpu.VMEM)
    smem = pl.BlockSpec(memory_space=pltpu.SMEM)
    hbm = pl.BlockSpec(memory_space=pltpu.HBM)
    bf16 = jnp.bfloat16
    dma = pltpu.SemaphoreType.DMA
    out = pl.pallas_call(
        kernel,
        out_shape=pltpu.VMEM((N_COL, N_ROW, R, R), jnp.float32),
        in_specs=[smem, smem, hbm, hbm, hbm],
        out_specs=vmem,
        scratch_shapes=[
            pltpu.VMEM((NP, PART, R), bf16),
            pltpu.VMEM((NP, PART, R), bf16),
            pltpu.VMEM((B, R), bf16),
            pltpu.VMEM((B, B), bf16),
            pltpu.VMEM((8, R), jnp.int32),
            pltpu.VMEM((N_ROW, 8, R), jnp.int32),
            pltpu.VMEM((8, R), jnp.int32),
            pltpu.VMEM((N_COL, 8, R), jnp.int32),
            pltpu.VMEM((N_ROW, B, R), bf16),
            pltpu.VMEM((N_COL, R, B), bf16),
            dma((128,)),
            dma((3,)),
            dma((N_ROW,)),
            dma((N_ROW,)),
            dma((N_COL,)),
            dma((1,)),
            dma((1,)),
            dma((N_ROW, CUTS)),
            dma((N_COL, CUTS)),
        ],
        compiler_params=pltpu.CompilerParams(
            collective_id=0, has_side_effects=True, vmem_limit_bytes=48 << 20),
        cost_estimate=pl.CostEstimate(
            flops=2 * grams * B, bytes_accessed=4 * grams * 2, transcendentals=0),
    )(owner_map, ranks, panel_right, factor_inverse, cores.reshape(N_COL, N_ROW, R, R))
    return out.reshape(cores.shape)


def solution(mesh):
    return jax.shard_map(
        body,
        mesh=mesh,
        in_specs=(
            P("row", "col", None),
            P(),
            P(("row", "col")),
            P(),
            P("row", "col", None, None, None, None),
        ),
        out_specs=P("row", "col", None, None, None, None),
        check_vma=False,
    )
```

```python
import jax
import jax.numpy as jnp
from jax import lax
from jax.experimental import pallas as pl
from jax.experimental.pallas import tpu as pltpu
from jax.sharding import PartitionSpec as P

B = 1536
R = 128
NP = 128
N_ROW = 8
N_COL = 16
ROWS = B // N_COL
PART = 16
PARTS = ROWS // PART
CUTS = 4
MESH = pl.DeviceIdType.MESH
NEAR, FAR, FLIP, RELAY, SHARE, WAIT, GRAM = range(7)
RIGHT, LEFT = 0, 1
Z_ORDER = (
    (LEFT, 0), (RIGHT, 0), (LEFT, 2), (RIGHT, 2), (LEFT, 1), (RIGHT, 1), (LEFT, 3), (RIGHT, 3),
)
STEPS = (
    (NEAR, RIGHT, 0, 1, 1), (FLIP, LEFT, 0), (FLIP, LEFT, 2), (NEAR, RIGHT, 0, -1, 2),
    (NEAR, LEFT, 0, -1, 3), (NEAR, LEFT, 0, 1, 0), (NEAR, LEFT, 0, -1, 2), (FLIP, RIGHT, 2),
    (FLIP, RIGHT, 0), (NEAR, LEFT, 0, 1, 1), (FLIP, LEFT, 1), (NEAR, LEFT, 0, -1, 0),
    (NEAR, RIGHT, 0, 1, 3), (NEAR, LEFT, 1, -1, 0), (FLIP, RIGHT, 1), (NEAR, LEFT, 0, 1, 2),
    (NEAR, RIGHT, 1, 1, 2), (NEAR, LEFT, 0, -1, 1), (FLIP, LEFT, 3), (NEAR, LEFT, 0, 1, 3),
    (NEAR, RIGHT, 0, -1, 1), (NEAR, RIGHT, 0, 1, 0), (NEAR, RIGHT, 0, -1, 3), (NEAR, LEFT, 1, 1, 0),
    (SHARE, 3, 0), (SHARE, 1, 0), (RELAY, 3), (SHARE, 0, 1),
    (FLIP, RIGHT, 3), (FAR, LEFT, 0), (RELAY, 1), (NEAR, LEFT, 1, -1, 2),
    (NEAR, RIGHT, 1, -1, 2), (SHARE, 2, 0), (WAIT, 0, 0), (NEAR, RIGHT, 0, 1, 2),
    (WAIT, 0, 1), (NEAR, RIGHT, 1, -1, 1), (NEAR, LEFT, 1, 1, 2), (FAR, RIGHT, 0),
    (NEAR, RIGHT, 0, -1, 0), (NEAR, RIGHT, 1, 1, 0), (WAIT, 1, 0), (NEAR, LEFT, 1, -1, 1),
    (NEAR, RIGHT, 1, -1, 0), (GRAM, 0, 1, 0), (NEAR, LEFT, 1, 1, 1), (WAIT, 3, 0),
    (GRAM, 1, 0, 0), (GRAM, 3, 0, 1), (WAIT, 2, 0), (GRAM, 0, 0, 0),
    (GRAM, 0, 0, 1), (NEAR, LEFT, 1, 1, 3), (GRAM, 2, 0, 0), (NEAR, LEFT, 1, -1, 3),
    (SHARE, 1, 1), (SHARE, 3, 1), (NEAR, RIGHT, 1, -1, 3), (NEAR, RIGHT, 1, 1, 3),
    (NEAR, RIGHT, 1, 1, 1), (GRAM, 1, 0, 1), (GRAM, 0, 1, 2), (GRAM, 0, 1, 1),
    (GRAM, 0, 0, 2), (GRAM, 2, 0, 2), (FAR, LEFT, 1), (SHARE, 2, 1),
    (GRAM, 3, 0, 0), (GRAM, 1, 0, 2), (GRAM, 2, 0, 1), (GRAM, 3, 0, 2),
    (WAIT, 3, 1), (WAIT, 1, 1), (GRAM, 1, 1, 1), (GRAM, 1, 1, 0),
    (GRAM, 3, 1, 1), (GRAM, 3, 1, 0), (FAR, RIGHT, 1), (WAIT, 2, 1),
)


def pair_at(y, zl, dy, flip):
    return ((y + dy) % 4) * 2 + (1 - zl if flip else zl)


def rights_at(x, zh):
    def row_of(dx, flip):
        return ((x + dx) % 4) * 2 + (1 - zh if flip else zh)

    return (
        (row_of(-1, 0), row_of(1, 0)),
        (row_of(0, 0), row_of(2, 0)),
        (row_of(-1, 1), row_of(1, 1)),
        (row_of(0, 1), row_of(2, 1)),
    )


def gram(left, right, out, pair, first, second):
    lhs = left[pl.ds(pair * 2, 2)].reshape(2 * R, B)
    rhs = jnp.concatenate([right[first], right[second]], axis=1)
    g = jnp.dot(lhs, rhs, preferred_element_type=jnp.float32)
    for i in range(2):
        for j, slot in enumerate((first, second)):
            out[pair * 2 + i, slot] -= g[i * R:(i + 1) * R, j * R:(j + 1) * R]


def finish(left, right, grams_in, out_hbm, grams, sem):
    r = lax.axis_index("row")
    c = lax.axis_index("col")
    x, zh, y, zl = r // 2, r % 2, c // 4, (c // 2) % 2
    done = {step[1:] for step in STEPS if step[0] == GRAM}
    copies = []
    for dy, flip in ((0, 0), (0, 1), (1, 0), (3, 0), (2, 0), (1, 1), (3, 1), (2, 1)):
        pair = pair_at(y, zl, dy, flip)
        for pick, rights in enumerate(rights_at(x, zh)):
            if (dy, flip, pick) not in done:
                gram(left, right, grams, pair, *rights)
        rows = pl.ds(pair * 2, 2)
        copy = pltpu.make_async_copy(grams.at[rows], out_hbm.at[rows], sem.at[len(copies)])
        copy.start()
        copies.append(copy)
    for copy in copies:
        copy.wait()


def kernel(owner_ref, rank_ref, panel_hbm, inverse_hbm, cores_hbm, out_ref, right, left,
           spread, moved, held, inverse, rank_mine, rank_rows, rank_pack, rank_all,
           send_sem, local_sem, sem_spread, sem_rank_a, sem_rank_b, sem_moved, sem_rows,
           sem_right, sem_left):
    r = lax.axis_index("row")
    c = lax.axis_index("col")
    x, zh = r // 2, r % 2
    y, zl, h = c // 4, (c // 2) % 2, c % 2

    inverse_copy = pltpu.make_async_copy(inverse_hbm, inverse, local_sem.at[0])
    cores_copy = pltpu.make_async_copy(cores_hbm, out_ref, local_sem.at[1])

    barrier = pltpu.get_barrier_semaphore()
    for d in range(1, N_ROW):
        pl.semaphore_signal(barrier, inc=1, device_id={"row": (r + d) % N_ROW, "col": c}, device_id_type=MESH)
    for d in range(1, N_COL):
        pl.semaphore_signal(barrier, inc=1, device_id={"row": r, "col": (c + d) % N_COL}, device_id_type=MESH)
    pl.semaphore_wait(barrier, N_ROW + N_COL - 2)

    sends = []
    counter = [0]

    def send(src, dst, recv, row, col, when=None):
        desc = pltpu.make_async_remote_copy(
            src_ref=src, dst_ref=dst, send_sem=send_sem.at[counter[0]], recv_sem=recv,
            device_id={"row": row, "col": col}, device_id_type=MESH)
        counter[0] += 1
        if when is None:
            desc.start()
        else:
            pl.when(when)(desc.start)
        sends.append((desc, when))

    def arrived(dst, recv):
        pltpu.make_async_remote_copy(
            src_ref=dst, dst_ref=dst, send_sem=recv, recv_sem=recv,
            device_id={"row": r, "col": c}, device_id_type=MESH).wait_recv()

    my_part = (r - c - 1) % N_ROW
    active = my_part < PARTS
    for d in range(1, N_ROW):
        to = (r + d) % N_ROW
        part = (to - c - 1) % N_ROW
        send(panel_hbm.at[:, pl.ds(pl.multiple_of(jnp.minimum(part, PARTS - 1) * PART, PART), PART), :],
             spread.at[pl.ds(r * N_COL, N_COL)], sem_spread.at[r], to, c, part < PARTS)
    own_part = pl.ds(pl.multiple_of(jnp.minimum(my_part, PARTS - 1) * PART, PART), PART)
    own_spread = pltpu.make_async_copy(
        panel_hbm.at[:, own_part, :], spread.at[pl.ds(r * N_COL, N_COL)], local_sem.at[2])
    pl.when(active)(own_spread.start)
    inverse_copy.start()

    rank_mine[...] = jnp.full((8, R), rank_ref[0], jnp.int32)
    for d in range(1, N_ROW):
        send(rank_mine, rank_rows.at[r], sem_rank_a.at[r], (r + d) % N_ROW, c)
    rank_rows[r] = rank_mine[...]

    @pl.when(active)
    def _():
        own_spread.wait()
        for d in range(1, N_ROW):
            frm = (r + d) % N_ROW
            arrived(spread.at[pl.ds(frm * N_COL, N_COL)], sem_spread.at[frm])

    for d in range(1, N_ROW):
        frm = (r + d) % N_ROW
        arrived(rank_rows.at[frm], sem_rank_a.at[frm])
    me = r * N_COL + c
    own_rows = pl.ds(pl.multiple_of(c * ROWS + jnp.minimum(my_part, PARTS - 1) * PART, PART), PART)
    own_copy = pltpu.make_async_copy(moved.at[me], held.at[own_rows, :], local_sem.at[2])

    @pl.when(active)
    def _():
        @pl.loop(1, NP)
        def _(d):
            p = (me + d) % NP
            moved[p] = spread[owner_ref[p]]
            pltpu.make_async_remote_copy(
                src_ref=moved.at[p], dst_ref=held.at[own_rows, :],
                send_sem=sem_moved.at[0], recv_sem=sem_rows.at[0],
                device_id={"row": p // N_COL, "col": p % N_COL}, device_id_type=MESH).start()
        moved[me] = spread[owner_ref[me]]
        own_copy.start()

    cores_copy.start()

    for k in range(N_ROW):
        rank_pack[pl.ds(k, 1), :] = rank_rows[k, pl.ds(0, 1), :]
    for d in range(1, N_COL):
        send(rank_pack, rank_all.at[c], sem_rank_b.at[c], r, (c + d) % N_COL)
    rank_all[c] = rank_pack[...]
    for d in range(1, N_COL):
        frm = (c + d) % N_COL
        arrived(rank_all.at[frm], sem_rank_b.at[frm])
    inverse_copy.wait()

    @pl.when(active)
    def _():
        own_copy.wait()
        arrived(held.at[pl.ds(0, B - PART), :], sem_rows.at[0])

    @pl.when(jnp.logical_not(active))
    def _():
        arrived(held, sem_rows.at[0])

    block = owner_ref[r * N_COL + c]
    rank = rank_all[block % N_COL, pl.ds(block // N_COL, 1), :]
    keep = lax.broadcasted_iota(jnp.int32, (1, R), 1) < rank
    step = 256
    for i in range(B // step):
        rows = slice(i * step, (i + 1) * step)
        done = (i + 1) * step
        solved = jnp.dot(inverse[rows, :done], held[:done, :], preferred_element_type=jnp.float32)
        solved = jnp.where(keep, solved, 0.0)
        right[r, rows, :] = solved.astype(jnp.bfloat16)
        left[c, :, rows] = solved.T.astype(jnp.bfloat16)

    def row_of(dx, flip):
        return ((x + dx) % 4) * 2 + (1 - zh if flip else zh)

    def col_of(dy, flip, other=0):
        return ((y + dy) % 4) * 4 + (1 - zl if flip else zl) * 2 + (1 - h if other else h)

    sibling = col_of(0, 0, 1)

    def half(ref, slot, part):
        size = ref.shape[1] // CUTS
        return ref.at[slot, pl.ds(part * size, size), :]

    def send_right(slot, part, dx, flip=0):
        ref = half(right, slot, part)
        send(ref, ref, sem_right.at[slot, part], row_of(dx, flip), c)

    def send_left(slot, part, dy, flip=0):
        ref = half(left, slot, part)
        send(ref, ref, sem_left.at[slot, part], r, col_of(dy, flip))

    def share(slot):
        send(left.at[slot], left.at[slot], sem_left.at[slot, 0], r, sibling)

    def wait_right(slot, part):
        arrived(half(right, slot, part), sem_right.at[slot, part])

    def wait_left(slot, part):
        arrived(half(left, slot, part), sem_left.at[slot, part])

    def wait_shared(slot):
        arrived(left.at[slot], sem_left.at[slot, 0])

    r_q, c_q = row_of(0, 1), col_of(0, 1)
    z_order = list(Z_ORDER)

    def along_z(count):
        for kind, part in z_order[:count]:
            if kind == RIGHT:
                send_right(r, part, 0, 1)
            else:
                send_left(c, part, 0, 1)
        del z_order[:count]

    along_z(2)
    for step in range(CUTS):
        for first, d in ((0, 1), (2, -1)):
            send_right(r, (first + step) % CUTS, d)
            send_left(c, (first + step) % CUTS, d)
        if step:
            along_z(2)
    share(c)
    cores_copy.wait()

    for step, *rest in STEPS:
        if step == NEAR:
            kind, flip, d, part = rest
            on = part // 2 == (0 if d == 1 else 1)
            if kind == RIGHT:
                wait_right(row_of(-d, flip), part)
                if on:
                    send_right(row_of(-d, flip), part, d)
            else:
                wait_left(col_of(-d, flip), part)
                if on and not (flip and part % 2):
                    send_left(col_of(-d, flip), part, d)
        elif step == FLIP:
            kind, part = rest
            if kind == RIGHT:
                wait_right(r_q, part)
            else:
                wait_left(c_q, part)
            for d in (1, -1):
                if kind == RIGHT:
                    send_right(r_q, part, d)
                else:
                    send_left(c_q, part, d)
        elif step == RELAY:
            wait_left(col_of(2, 0), rest[0])
            send_left(col_of(2, 0), rest[0], 0, 1)
        elif step == FAR:
            kind, flip = rest
            for part in range(CUTS):
                if kind == RIGHT:
                    wait_right(row_of(2, flip), part)
                elif flip or part % 2 == 0:
                    wait_left(col_of(2, flip), part)
        elif step == SHARE:
            share(col_of(*rest))
        elif step == WAIT:
            wait_shared(col_of(*rest, 1))
        else:
            dy, flip, pick = rest
            gram(left, right, out_ref, pair_at(y, zl, dy, flip), *rights_at(x, zh)[pick])

    @pl.when(active)
    def _():
        pltpu.make_async_remote_copy(
            src_ref=moved.at[pl.ds(0, NP - 1)], dst_ref=moved.at[pl.ds(0, NP - 1)],
            send_sem=sem_moved.at[0], recv_sem=sem_moved.at[0],
            device_id={"row": r, "col": c}, device_id_type=MESH).wait_send()

    for desc, when in sends:
        if when is None:
            desc.wait_send()
        else:
            pl.when(when)(desc.wait_send)


def body(panel_right, factor_inverse, ranks, owner_map, cores):
    grams = 16 * 8 * 128 * 128
    vmem = pl.BlockSpec(memory_space=pltpu.VMEM)
    smem = pl.BlockSpec(memory_space=pltpu.SMEM)
    hbm = pl.BlockSpec(memory_space=pltpu.HBM)
    bf16 = jnp.bfloat16
    dma = pltpu.SemaphoreType.DMA
    out, right, left = pl.pallas_call(
        kernel,
        out_shape=(
            pltpu.VMEM((N_COL, N_ROW, R, R), jnp.float32),
            pltpu.VMEM((N_ROW, B, R), bf16),
            pltpu.VMEM((N_COL, R, B), bf16),
        ),
        in_specs=[smem, smem, hbm, hbm, hbm],
        out_specs=(vmem, vmem, vmem),
        scratch_shapes=[
            pltpu.VMEM((NP, PART, R), bf16),
            pltpu.VMEM((NP, PART, R), bf16),
            pltpu.VMEM((B, R), bf16),
            pltpu.VMEM((B, B), bf16),
            pltpu.VMEM((8, R), jnp.int32),
            pltpu.VMEM((N_ROW, 8, R), jnp.int32),
            pltpu.VMEM((8, R), jnp.int32),
            pltpu.VMEM((N_COL, 8, R), jnp.int32),
            dma((128,)),
            dma((3,)),
            dma((N_ROW,)),
            dma((N_ROW,)),
            dma((N_COL,)),
            dma((1,)),
            dma((1,)),
            dma((N_ROW, CUTS)),
            dma((N_COL, CUTS)),
        ],
        compiler_params=pltpu.CompilerParams(
            collective_id=0, has_side_effects=True, vmem_limit_bytes=(46 << 20) + (512 << 10)),
        cost_estimate=pl.CostEstimate(
            flops=2 * grams * B, bytes_accessed=4 * grams * 2, transcendentals=0),
    )(owner_map, ranks, panel_right, factor_inverse, cores.reshape(N_COL, N_ROW, R, R))
    here = [pltpu.with_memory_space_constraint(v, pltpu.VMEM) for v in (left, right, out)]
    out, _ = pl.pallas_call(
        finish,
        out_shape=(jax.ShapeDtypeStruct(out.shape, jnp.float32), pltpu.VMEM(out.shape, jnp.float32)),
        in_specs=[vmem, vmem, vmem],
        out_specs=(hbm, vmem),
        input_output_aliases={2: 1},
        scratch_shapes=[dma((N_COL // 2,))],
        compiler_params=pltpu.CompilerParams(vmem_limit_bytes=8 << 20),
    )(*here)
    return out.reshape(cores.shape)


def solution(mesh):
    return jax.shard_map(
        body,
        mesh=mesh,
        in_specs=(
            P("row", "col", None),
            P(),
            P(("row", "col")),
            P(),
            P("row", "col", None, None, None, None),
        ),
        out_specs=P("row", "col", None, None, None, None),
        check_vma=False,
    )
```

```python
import jax
import jax.numpy as jnp
from jax import lax
from jax.experimental import pallas as pl
from jax.experimental.pallas import tpu as pltpu
from jax.sharding import PartitionSpec as P

B = 1536
R = 128
NP = 128
N_ROW = 8
N_COL = 16
ROWS = B // N_COL
PART = 16
PARTS = ROWS // PART
CUTS = 4
MESH = pl.DeviceIdType.MESH
NEAR, FAR, FLIP, RELAY, SHARE, WAIT, GRAM = range(7)
RIGHT, LEFT = 0, 1
Z_ORDER = (
    (LEFT, 0), (RIGHT, 0), (LEFT, 2), (RIGHT, 2), (LEFT, 1), (RIGHT, 1), (LEFT, 3), (RIGHT, 3),
)
STEPS = (
    (NEAR, RIGHT, 0, 1, 1), (FLIP, LEFT, 0), (FLIP, LEFT, 2), (NEAR, RIGHT, 0, -1, 2),
    (NEAR, LEFT, 0, -1, 3), (NEAR, LEFT, 0, 1, 0), (NEAR, LEFT, 0, -1, 2), (FLIP, RIGHT, 2),
    (FLIP, RIGHT, 0), (NEAR, LEFT, 0, 1, 1), (FLIP, LEFT, 1), (NEAR, LEFT, 0, -1, 0),
    (NEAR, RIGHT, 0, 1, 3), (NEAR, LEFT, 1, -1, 0), (FLIP, RIGHT, 1), (NEAR, LEFT, 0, 1, 2),
    (NEAR, RIGHT, 1, 1, 2), (NEAR, LEFT, 0, -1, 1), (FLIP, LEFT, 3), (NEAR, LEFT, 0, 1, 3),
    (NEAR, RIGHT, 0, -1, 1), (NEAR, RIGHT, 0, 1, 0), (NEAR, RIGHT, 0, -1, 3), (NEAR, LEFT, 1, 1, 0),
    (SHARE, 3, 0), (SHARE, 1, 0), (RELAY, 3), (SHARE, 0, 1),
    (FLIP, RIGHT, 3), (FAR, LEFT, 0), (RELAY, 1), (NEAR, LEFT, 1, -1, 2),
    (NEAR, RIGHT, 1, -1, 2), (SHARE, 2, 0), (WAIT, 0, 0), (NEAR, RIGHT, 0, 1, 2),
    (WAIT, 0, 1), (NEAR, RIGHT, 1, -1, 1), (NEAR, LEFT, 1, 1, 2), (FAR, RIGHT, 0),
    (NEAR, RIGHT, 0, -1, 0), (NEAR, RIGHT, 1, 1, 0), (WAIT, 1, 0), (NEAR, LEFT, 1, -1, 1),
    (NEAR, RIGHT, 1, -1, 0), (GRAM, 0, 1, 0), (NEAR, LEFT, 1, 1, 1), (WAIT, 3, 0),
    (GRAM, 1, 0, 0), (GRAM, 3, 0, 1), (WAIT, 2, 0), (GRAM, 0, 0, 0),
    (GRAM, 0, 0, 1), (NEAR, LEFT, 1, 1, 3), (GRAM, 2, 0, 0), (NEAR, LEFT, 1, -1, 3),
    (SHARE, 1, 1), (SHARE, 3, 1), (NEAR, RIGHT, 1, -1, 3), (NEAR, RIGHT, 1, 1, 3),
    (NEAR, RIGHT, 1, 1, 1), (GRAM, 1, 0, 1), (GRAM, 0, 1, 2), (GRAM, 0, 1, 1),
    (GRAM, 0, 0, 2), (GRAM, 2, 0, 2), (FAR, LEFT, 1), (SHARE, 2, 1),
    (GRAM, 3, 0, 0), (GRAM, 1, 0, 2), (GRAM, 2, 0, 1), (GRAM, 3, 0, 2),
    (WAIT, 3, 1), (WAIT, 1, 1), (GRAM, 1, 1, 1), (GRAM, 1, 1, 0),
    (GRAM, 3, 1, 1), (GRAM, 3, 1, 0), (FAR, RIGHT, 1), (WAIT, 2, 1),
)


def pair_at(y, zl, dy, flip):
    return ((y + dy) % 4) * 2 + (1 - zl if flip else zl)


def rights_at(x, zh):
    def row_of(dx, flip):
        return ((x + dx) % 4) * 2 + (1 - zh if flip else zh)

    return (
        (row_of(-1, 0), row_of(1, 0)),
        (row_of(0, 0), row_of(2, 0)),
        (row_of(-1, 1), row_of(1, 1)),
        (row_of(0, 1), row_of(2, 1)),
    )


def gram(left, right, out, pair, first, second):
    lhs = left[pl.ds(pair * 2, 2)].reshape(2 * R, B)
    rhs = jnp.concatenate([right[first], right[second]], axis=1)
    g = jnp.dot(lhs, rhs, preferred_element_type=jnp.float32)
    for i in range(2):
        for j, slot in enumerate((first, second)):
            out[pair * 2 + i, slot] -= g[i * R:(i + 1) * R, j * R:(j + 1) * R]


def finish(left, right, grams_in, out_hbm, grams, sem):
    r = lax.axis_index("row")
    c = lax.axis_index("col")
    x, zh, y, zl = r // 2, r % 2, c // 4, (c // 2) % 2
    done = {step[1:] for step in STEPS if step[0] == GRAM}
    copies = []
    for dy, flip in ((0, 0), (0, 1), (1, 0), (3, 0), (2, 0), (1, 1), (3, 1), (2, 1)):
        pair = pair_at(y, zl, dy, flip)
        for pick, rights in enumerate(rights_at(x, zh)):
            if (dy, flip, pick) not in done:
                gram(left, right, grams, pair, *rights)
        rows = pl.ds(pair * 2, 2)
        copy = pltpu.make_async_copy(grams.at[rows], out_hbm.at[rows], sem.at[len(copies)])
        copy.start()
        copies.append(copy)
    for copy in copies:
        copy.wait()


def kernel(owner_hbm, rank_hbm, panel_hbm, inverse_hbm, cores_hbm, out_ref, right, left,
           owner_ref, rank_ref, panel, spread, moved, held, inverse, rank_mine, rank_rows, rank_pack, rank_all,
           send_sem, local_sem, sem_spread, sem_rank_a, sem_rank_b, sem_moved, sem_rows,
           sem_right, sem_left):
    r = lax.axis_index("row")
    c = lax.axis_index("col")
    x, zh = r // 2, r % 2
    y, zl, h = c // 4, (c // 2) % 2, c % 2

    barrier = pltpu.get_barrier_semaphore()
    for d in range(1, N_ROW):
        pl.semaphore_signal(barrier, inc=1, device_id={"row": (r + d) % N_ROW, "col": c}, device_id_type=MESH)
    for d in range(1, N_COL):
        pl.semaphore_signal(barrier, inc=1, device_id={"row": r, "col": (c + d) % N_COL}, device_id_type=MESH)
    inverse_copy = pltpu.make_async_copy(inverse_hbm, inverse, local_sem.at[0])
    cores_copy = pltpu.make_async_copy(cores_hbm, out_ref, local_sem.at[1])
    panel_copy = pltpu.make_async_copy(panel_hbm, panel, local_sem.at[3])
    rank_copy = pltpu.make_async_copy(rank_hbm, rank_ref, local_sem.at[4])
    owner_copy = pltpu.make_async_copy(owner_hbm, owner_ref, local_sem.at[5])
    for copy in (panel_copy, rank_copy, owner_copy):
        copy.start()
    panel_copy.wait()
    pl.semaphore_wait(barrier, N_ROW + N_COL - 2)

    SPREAD, RANK_A, RANK_B, TO_ROW, TO_COL = range(5)
    sent = [0] * 5

    def send(src, dst, recv, row, col, group, when=None):
        desc = pltpu.make_async_remote_copy(
            src_ref=src, dst_ref=dst, send_sem=send_sem.at[group], recv_sem=recv,
            device_id={"row": row, "col": col}, device_id_type=MESH)
        sent[group] += src.shape[-3] if len(src.shape) == 3 else src.shape[-2]
        if when is None:
            desc.start()
        else:
            pl.when(when)(desc.start)

    def left_device(ref, sem):
        pltpu.make_async_remote_copy(
            src_ref=ref, dst_ref=ref, send_sem=sem, recv_sem=sem,
            device_id={"row": r, "col": c}, device_id_type=MESH).wait_send()

    def arrived(dst, recv):
        pltpu.make_async_remote_copy(
            src_ref=dst, dst_ref=dst, send_sem=recv, recv_sem=recv,
            device_id={"row": r, "col": c}, device_id_type=MESH).wait_recv()

    my_part = (r - c - 1) % N_ROW
    active = my_part < PARTS
    for d in range(1, N_ROW):
        to = (r + d) % N_ROW
        part = (to - c - 1) % N_ROW
        send(panel.at[:, pl.ds(pl.multiple_of(jnp.minimum(part, PARTS - 1) * PART, PART), PART), :],
             spread.at[pl.ds(r * N_COL, N_COL)], sem_spread.at[r], to, c, SPREAD, part < PARTS)
    own_part = pl.ds(pl.multiple_of(jnp.minimum(my_part, PARTS - 1) * PART, PART), PART)
    own_spread = pltpu.make_async_copy(
        panel.at[:, own_part, :], spread.at[pl.ds(r * N_COL, N_COL)], local_sem.at[2])
    pl.when(active)(own_spread.start)
    inverse_copy.start()

    rank_copy.wait()
    rank_mine[...] = jnp.full((8, R), rank_ref[0], jnp.int32)
    for d in range(1, N_ROW):
        send(rank_mine, rank_rows.at[r], sem_rank_a.at[r], (r + d) % N_ROW, c, RANK_A)
    rank_rows[r] = rank_mine[...]
    owner_copy.wait()

    @pl.when(active)
    def _():
        own_spread.wait()
        for d in range(1, N_ROW):
            frm = (r + d) % N_ROW
            arrived(spread.at[pl.ds(frm * N_COL, N_COL)], sem_spread.at[frm])

    me = r * N_COL + c
    own_rows = pl.ds(pl.multiple_of(c * ROWS + jnp.minimum(my_part, PARTS - 1) * PART, PART), PART)
    own_copy = pltpu.make_async_copy(moved.at[me], held.at[own_rows, :], local_sem.at[2])

    @pl.when(active)
    def _():
        @pl.loop(1, NP)
        def _(d):
            p = (me + d) % NP
            moved[p] = spread[owner_ref[p]]
            pltpu.make_async_remote_copy(
                src_ref=moved.at[p], dst_ref=held.at[own_rows, :],
                send_sem=sem_moved.at[0], recv_sem=sem_rows.at[0],
                device_id={"row": p // N_COL, "col": p % N_COL}, device_id_type=MESH).start()
        moved[me] = spread[owner_ref[me]]
        own_copy.start()

    cores_copy.start()

    for d in range(1, N_ROW):
        frm = (r + d) % N_ROW
        arrived(rank_rows.at[frm], sem_rank_a.at[frm])
    for k in range(N_ROW):
        rank_pack[pl.ds(k, 1), :] = rank_rows[k, pl.ds(0, 1), :]
    for d in range(1, N_COL):
        send(rank_pack, rank_all.at[c], sem_rank_b.at[c], r, (c + d) % N_COL, RANK_B)
    rank_all[c] = rank_pack[...]
    for d in range(1, N_COL):
        frm = (c + d) % N_COL
        arrived(rank_all.at[frm], sem_rank_b.at[frm])
    inverse_copy.wait()

    @pl.when(active)
    def _():
        own_copy.wait()
        arrived(held.at[pl.ds(0, B - PART), :], sem_rows.at[0])

    @pl.when(jnp.logical_not(active))
    def _():
        arrived(held, sem_rows.at[0])

    block = owner_ref[r * N_COL + c]
    rank = rank_all[block % N_COL, pl.ds(block // N_COL, 1), :]
    keep = lax.broadcasted_iota(jnp.int32, (1, R), 1) < rank
    step = 256
    for i in range(B // step):
        rows = slice(i * step, (i + 1) * step)
        done = (i + 1) * step
        solved = jnp.dot(inverse[rows, :done], held[:done, :], preferred_element_type=jnp.float32)
        solved = jnp.where(keep, solved, 0.0)
        right[r, rows, :] = solved.astype(jnp.bfloat16)
        left[c, :, rows] = solved.T.astype(jnp.bfloat16)

    def row_of(dx, flip):
        return ((x + dx) % 4) * 2 + (1 - zh if flip else zh)

    def col_of(dy, flip, other=0):
        return ((y + dy) % 4) * 4 + (1 - zl if flip else zl) * 2 + (1 - h if other else h)

    sibling = col_of(0, 0, 1)

    def half(ref, slot, part):
        size = ref.shape[1] // CUTS
        return ref.at[slot, pl.ds(part * size, size), :]

    def send_right(slot, part, dx, flip=0):
        ref = half(right, slot, part)
        send(ref, ref, sem_right.at[slot, part], row_of(dx, flip), c, TO_ROW)

    def send_left(slot, part, dy, flip=0):
        ref = half(left, slot, part)
        send(ref, ref, sem_left.at[slot, part], r, col_of(dy, flip), TO_COL)

    def share(slot):
        send(left.at[slot], left.at[slot], sem_left.at[slot, 0], r, sibling, TO_COL)

    def wait_right(slot, part):
        arrived(half(right, slot, part), sem_right.at[slot, part])

    def wait_left(slot, part):
        arrived(half(left, slot, part), sem_left.at[slot, part])

    def wait_shared(slot):
        arrived(left.at[slot], sem_left.at[slot, 0])

    r_q, c_q = row_of(0, 1), col_of(0, 1)
    z_order = list(Z_ORDER)

    def along_z(count):
        for kind, part in z_order[:count]:
            if kind == RIGHT:
                send_right(r, part, 0, 1)
            else:
                send_left(c, part, 0, 1)
        del z_order[:count]

    along_z(2)
    for step in range(CUTS):
        for first, d in ((0, 1), (2, -1)):
            send_right(r, (first + step) % CUTS, d)
            send_left(c, (first + step) % CUTS, d)
        if step:
            along_z(2)
    share(c)
    cores_copy.wait()

    for step, *rest in STEPS:
        if step == NEAR:
            kind, flip, d, part = rest
            on = part // 2 == (0 if d == 1 else 1)
            if kind == RIGHT:
                wait_right(row_of(-d, flip), part)
                if on:
                    send_right(row_of(-d, flip), part, d)
            else:
                wait_left(col_of(-d, flip), part)
                if on and not (flip and part % 2):
                    send_left(col_of(-d, flip), part, d)
        elif step == FLIP:
            kind, part = rest
            if kind == RIGHT:
                wait_right(r_q, part)
            else:
                wait_left(c_q, part)
            for d in (1, -1):
                if kind == RIGHT:
                    send_right(r_q, part, d)
                else:
                    send_left(c_q, part, d)
        elif step == RELAY:
            wait_left(col_of(2, 0), rest[0])
            send_left(col_of(2, 0), rest[0], 0, 1)
        elif step == FAR:
            kind, flip = rest
            for part in range(CUTS):
                if kind == RIGHT:
                    wait_right(row_of(2, flip), part)
                elif flip or part % 2 == 0:
                    wait_left(col_of(2, flip), part)
        elif step == SHARE:
            share(col_of(*rest))
        elif step == WAIT:
            wait_shared(col_of(*rest, 1))
        else:
            dy, flip, pick = rest
            gram(left, right, out_ref, pair_at(y, zl, dy, flip), *rights_at(x, zh)[pick])

    assert sent[TO_ROW] % B == 0 and sent[TO_COL] % R == 0

    @pl.when(active)
    def _():
        left_device(moved.at[pl.ds(0, NP - 1)], sem_moved.at[0])
        left_device(spread.at[pl.ds(0, (PARTS - 1) * N_COL)], send_sem.at[SPREAD])

    @pl.when(jnp.logical_not(active))
    def _():
        left_device(spread.at[pl.ds(0, PARTS * N_COL)], send_sem.at[SPREAD])

    left_device(rank_rows.at[pl.ds(0, N_ROW - 1)], send_sem.at[RANK_A])
    left_device(rank_all.at[pl.ds(0, N_COL - 1)], send_sem.at[RANK_B])
    left_device(right.at[pl.ds(0, sent[TO_ROW] // B)], send_sem.at[TO_ROW])
    left_device(left.at[pl.ds(0, sent[TO_COL] // R)], send_sem.at[TO_COL])


def body(panel_right, factor_inverse, ranks, owner_map, cores):
    grams = 16 * 8 * 128 * 128
    vmem = pl.BlockSpec(memory_space=pltpu.VMEM)
    hbm = pl.BlockSpec(memory_space=pltpu.HBM)
    bf16 = jnp.bfloat16
    dma = pltpu.SemaphoreType.DMA
    out, right, left = pl.pallas_call(
        kernel,
        out_shape=(
            pltpu.VMEM((N_COL, N_ROW, R, R), jnp.float32),
            pltpu.VMEM((N_ROW, B, R), bf16),
            pltpu.VMEM((N_COL, R, B), bf16),
        ),
        in_specs=[hbm, hbm, hbm, hbm, hbm],
        out_specs=(vmem, vmem, vmem),
        scratch_shapes=[
            pltpu.SMEM((NP,), jnp.int32),
            pltpu.SMEM((1,), jnp.int32),
            pltpu.VMEM((N_COL, ROWS, R), bf16),
            pltpu.VMEM((NP, PART, R), bf16),
            pltpu.VMEM((NP, PART, R), bf16),
            pltpu.VMEM((B, R), bf16),
            pltpu.VMEM((B, B), bf16),
            pltpu.VMEM((8, R), jnp.int32),
            pltpu.VMEM((N_ROW, 8, R), jnp.int32),
            pltpu.VMEM((8, R), jnp.int32),
            pltpu.VMEM((N_COL, 8, R), jnp.int32),
            dma((5,)),
            dma((6,)),
            dma((N_ROW,)),
            dma((N_ROW,)),
            dma((N_COL,)),
            dma((1,)),
            dma((1,)),
            dma((N_ROW, CUTS)),
            dma((N_COL, CUTS)),
        ],
        compiler_params=pltpu.CompilerParams(
            collective_id=0, has_side_effects=True, vmem_limit_bytes=(46 << 20) + (512 << 10)),
        cost_estimate=pl.CostEstimate(
            flops=2 * grams * B, bytes_accessed=4 * grams * 2, transcendentals=0),
    )(owner_map, ranks, panel_right, factor_inverse, cores.reshape(N_COL, N_ROW, R, R))
    here = [pltpu.with_memory_space_constraint(v, pltpu.VMEM) for v in (left, right, out)]
    out, _ = pl.pallas_call(
        finish,
        out_shape=(jax.ShapeDtypeStruct(out.shape, jnp.float32), pltpu.VMEM(out.shape, jnp.float32)),
        in_specs=[vmem, vmem, vmem],
        out_specs=(hbm, vmem),
        input_output_aliases={2: 1},
        scratch_shapes=[dma((N_COL // 2,))],
        compiler_params=pltpu.CompilerParams(vmem_limit_bytes=8 << 20),
    )(*here)
    return out.reshape(cores.shape)


def solution(mesh):
    return jax.shard_map(
        body,
        mesh=mesh,
        in_specs=(
            P("row", "col", None),
            P(),
            P(("row", "col")),
            P(),
            P("row", "col", None, None, None, None),
        ),
        out_specs=P("row", "col", None, None, None, None),
        check_vma=False,
    )
```

```python
import jax
import jax.numpy as jnp
from jax import lax
from jax.experimental import pallas as pl
from jax.experimental.pallas import tpu as pltpu
from jax.sharding import PartitionSpec as P

B = 1536
R = 128
NP = 128
N_ROW = 8
N_COL = 16
ROWS = B // N_COL
PART = 16
PARTS = ROWS // PART
CUTS = 4
MESH = pl.DeviceIdType.MESH
NEAR, FAR, FLIP, RELAY, SHARE, WAIT, GRAM = range(7)
RIGHT, LEFT = 0, 1
Z_ORDER = (
    (LEFT, 0), (RIGHT, 0), (LEFT, 2), (RIGHT, 2), (LEFT, 1), (RIGHT, 1), (LEFT, 3), (RIGHT, 3),
)
STEPS = (
    (NEAR, RIGHT, 0, 1, 1), (FLIP, LEFT, 0), (FLIP, LEFT, 2), (NEAR, RIGHT, 0, -1, 2),
    (NEAR, LEFT, 0, -1, 3), (NEAR, LEFT, 0, 1, 0), (NEAR, LEFT, 0, -1, 2), (FLIP, RIGHT, 2),
    (FLIP, RIGHT, 0), (NEAR, LEFT, 0, 1, 1), (FLIP, LEFT, 1), (NEAR, LEFT, 0, -1, 0),
    (NEAR, RIGHT, 0, 1, 3), (NEAR, LEFT, 1, -1, 0), (FLIP, RIGHT, 1), (NEAR, LEFT, 0, 1, 2),
    (NEAR, RIGHT, 1, 1, 2), (NEAR, LEFT, 0, -1, 1), (FLIP, LEFT, 3), (NEAR, LEFT, 0, 1, 3),
    (NEAR, RIGHT, 0, -1, 1), (NEAR, RIGHT, 0, 1, 0), (NEAR, RIGHT, 0, -1, 3), (NEAR, LEFT, 1, 1, 0),
    (SHARE, 3, 0), (SHARE, 1, 0), (RELAY, 3), (SHARE, 0, 1),
    (FLIP, RIGHT, 3), (FAR, LEFT, 0), (RELAY, 1), (NEAR, LEFT, 1, -1, 2),
    (NEAR, RIGHT, 1, -1, 2), (SHARE, 2, 0), (WAIT, 0, 0), (NEAR, RIGHT, 0, 1, 2),
    (WAIT, 0, 1), (NEAR, RIGHT, 1, -1, 1), (NEAR, LEFT, 1, 1, 2), (FAR, RIGHT, 0),
    (NEAR, RIGHT, 0, -1, 0), (NEAR, RIGHT, 1, 1, 0), (WAIT, 1, 0), (NEAR, LEFT, 1, -1, 1),
    (NEAR, RIGHT, 1, -1, 0), (GRAM, 0, 1, 0), (NEAR, LEFT, 1, 1, 1), (WAIT, 3, 0),
    (GRAM, 1, 0, 0), (GRAM, 3, 0, 1), (WAIT, 2, 0), (GRAM, 0, 0, 0),
    (GRAM, 0, 0, 1), (NEAR, LEFT, 1, 1, 3), (GRAM, 2, 0, 0), (NEAR, LEFT, 1, -1, 3),
    (SHARE, 1, 1), (SHARE, 3, 1), (NEAR, RIGHT, 1, -1, 3), (NEAR, RIGHT, 1, 1, 3),
    (NEAR, RIGHT, 1, 1, 1), (GRAM, 1, 0, 1), (GRAM, 0, 1, 2), (GRAM, 0, 1, 1),
    (GRAM, 0, 0, 2), (GRAM, 2, 0, 2), (FAR, LEFT, 1), (SHARE, 2, 1),
    (GRAM, 3, 0, 0), (GRAM, 1, 0, 2), (GRAM, 2, 0, 1), (GRAM, 3, 0, 2),
    (WAIT, 3, 1), (WAIT, 1, 1), (GRAM, 1, 1, 1), (GRAM, 1, 1, 0),
    (GRAM, 3, 1, 1), (GRAM, 3, 1, 0), (GRAM, 1, 1, 2), (GRAM, 3, 1, 2),
    (FAR, RIGHT, 1), (WAIT, 2, 1),
)


def pair_at(y, zl, dy, flip):
    return ((y + dy) % 4) * 2 + (1 - zl if flip else zl)


def rights_at(x, zh):
    def row_of(dx, flip):
        return ((x + dx) % 4) * 2 + (1 - zh if flip else zh)

    return (
        (row_of(-1, 0), row_of(1, 0)),
        (row_of(0, 0), row_of(2, 0)),
        (row_of(-1, 1), row_of(1, 1)),
        (row_of(0, 1), row_of(2, 1)),
    )


def gram(left, right, out, pair, first, second):
    lhs = left[pl.ds(pair * 2, 2)].reshape(2 * R, B)
    rhs = jnp.concatenate([right[first], right[second]], axis=1)
    g = jnp.dot(lhs, rhs, preferred_element_type=jnp.float32)
    for i in range(2):
        for j, slot in enumerate((first, second)):
            out[pair * 2 + i, slot] -= g[i * R:(i + 1) * R, j * R:(j + 1) * R]


def finish(left, right, grams_in, out_hbm, grams, sem):
    r = lax.axis_index("row")
    c = lax.axis_index("col")
    x, zh, y, zl = r // 2, r % 2, c // 4, (c // 2) % 2
    done = {step[1:] for step in STEPS if step[0] == GRAM}
    copies = []
    for dy, flip in ((0, 0), (0, 1), (1, 0), (3, 0), (2, 0), (1, 1), (3, 1), (2, 1)):
        pair = pair_at(y, zl, dy, flip)
        for pick, rights in enumerate(rights_at(x, zh)):
            if (dy, flip, pick) not in done:
                gram(left, right, grams, pair, *rights)
        rows = pl.ds(pair * 2, 2)
        copy = pltpu.make_async_copy(grams.at[rows], out_hbm.at[rows], sem.at[len(copies)])
        copy.start()
        copies.append(copy)
    for copy in copies:
        copy.wait()


def kernel(owner_hbm, rank_hbm, panel_hbm, inverse_hbm, cores_hbm, out_ref, right, left,
           owner_ref, rank_ref, panel, spread, moved, held, inverse, rank_mine, rank_rows, rank_pack, rank_all,
           send_sem, local_sem, sem_spread, sem_rank_a, sem_rank_b, sem_moved, sem_rows,
           sem_right, sem_left):
    r = lax.axis_index("row")
    c = lax.axis_index("col")
    x, zh = r // 2, r % 2
    y, zl, h = c // 4, (c // 2) % 2, c % 2

    panel_copy = pltpu.make_async_copy(panel_hbm, panel, local_sem.at[3])
    panel_copy.start()

    barrier = pltpu.get_barrier_semaphore()
    for d in range(1, N_ROW):
        pl.semaphore_signal(barrier, inc=1, device_id={"row": (r + d) % N_ROW, "col": c}, device_id_type=MESH)
    for d in range(1, N_COL):
        pl.semaphore_signal(barrier, inc=1, device_id={"row": r, "col": (c + d) % N_COL}, device_id_type=MESH)
    inverse_copy = pltpu.make_async_copy(inverse_hbm, inverse, local_sem.at[0])
    cores_copy = pltpu.make_async_copy(cores_hbm, out_ref, local_sem.at[1])
    rank_copy = pltpu.make_async_copy(rank_hbm, rank_ref, local_sem.at[4])
    owner_copy = pltpu.make_async_copy(owner_hbm, owner_ref, local_sem.at[5])
    for copy in (rank_copy, owner_copy):
        copy.start()
    panel_copy.wait()
    pl.semaphore_wait(barrier, N_ROW + N_COL - 2)

    SPREAD, RANK_A, RANK_B, TO_ROW, TO_COL = range(5)
    sent = [0] * 5

    def send(src, dst, recv, row, col, group, when=None):
        desc = pltpu.make_async_remote_copy(
            src_ref=src, dst_ref=dst, send_sem=send_sem.at[group], recv_sem=recv,
            device_id={"row": row, "col": col}, device_id_type=MESH)
        sent[group] += src.shape[-3] if len(src.shape) == 3 else src.shape[-2]
        if when is None:
            desc.start()
        else:
            pl.when(when)(desc.start)

    def left_device(ref, sem):
        pltpu.make_async_remote_copy(
            src_ref=ref, dst_ref=ref, send_sem=sem, recv_sem=sem,
            device_id={"row": r, "col": c}, device_id_type=MESH).wait_send()

    def arrived(dst, recv):
        pltpu.make_async_remote_copy(
            src_ref=dst, dst_ref=dst, send_sem=recv, recv_sem=recv,
            device_id={"row": r, "col": c}, device_id_type=MESH).wait_recv()

    my_part = (r - c - 1) % N_ROW
    active = my_part < PARTS
    for d in range(1, N_ROW):
        to = (r + d) % N_ROW
        part = (to - c - 1) % N_ROW
        send(panel.at[:, pl.ds(pl.multiple_of(jnp.minimum(part, PARTS - 1) * PART, PART), PART), :],
             spread.at[pl.ds(r * N_COL, N_COL)], sem_spread.at[r], to, c, SPREAD, part < PARTS)
    own_part = pl.ds(pl.multiple_of(jnp.minimum(my_part, PARTS - 1) * PART, PART), PART)
    own_spread = pltpu.make_async_copy(
        panel.at[:, own_part, :], spread.at[pl.ds(r * N_COL, N_COL)], local_sem.at[2])
    pl.when(active)(own_spread.start)
    inverse_copy.start()

    rank_copy.wait()
    rank_mine[...] = jnp.full((8, R), rank_ref[0], jnp.int32)
    for d in range(1, N_ROW):
        send(rank_mine, rank_rows.at[r], sem_rank_a.at[r], (r + d) % N_ROW, c, RANK_A)
    rank_rows[r] = rank_mine[...]
    owner_copy.wait()

    @pl.when(active)
    def _():
        own_spread.wait()
        for d in range(1, N_ROW):
            frm = (r + d) % N_ROW
            arrived(spread.at[pl.ds(frm * N_COL, N_COL)], sem_spread.at[frm])

    me = r * N_COL + c
    own_rows = pl.ds(pl.multiple_of(c * ROWS + jnp.minimum(my_part, PARTS - 1) * PART, PART), PART)
    own_copy = pltpu.make_async_copy(moved.at[me], held.at[own_rows, :], local_sem.at[2])

    @pl.when(active)
    def _():
        @pl.loop(1, NP)
        def _(d):
            p = (me + d) % NP
            moved[p] = spread[owner_ref[p]]
            pltpu.make_async_remote_copy(
                src_ref=moved.at[p], dst_ref=held.at[own_rows, :],
                send_sem=sem_moved.at[0], recv_sem=sem_rows.at[0],
                device_id={"row": p // N_COL, "col": p % N_COL}, device_id_type=MESH).start()
        moved[me] = spread[owner_ref[me]]
        own_copy.start()

    cores_copy.start()

    for d in range(1, N_ROW):
        frm = (r + d) % N_ROW
        arrived(rank_rows.at[frm], sem_rank_a.at[frm])
    for k in range(N_ROW):
        rank_pack[pl.ds(k, 1), :] = rank_rows[k, pl.ds(0, 1), :]
    for d in range(1, N_COL):
        send(rank_pack, rank_all.at[c], sem_rank_b.at[c], r, (c + d) % N_COL, RANK_B)
    rank_all[c] = rank_pack[...]
    for d in range(1, N_COL):
        frm = (c + d) % N_COL
        arrived(rank_all.at[frm], sem_rank_b.at[frm])
    inverse_copy.wait()

    @pl.when(active)
    def _():
        own_copy.wait()
        arrived(held.at[pl.ds(0, B - PART), :], sem_rows.at[0])

    @pl.when(jnp.logical_not(active))
    def _():
        arrived(held, sem_rows.at[0])

    block = owner_ref[r * N_COL + c]
    rank = rank_all[block % N_COL, pl.ds(block // N_COL, 1), :]
    keep = lax.broadcasted_iota(jnp.int32, (1, R), 1) < rank
    step = 256
    for i in range(B // step):
        rows = slice(i * step, (i + 1) * step)
        done = (i + 1) * step
        solved = jnp.dot(inverse[rows, :done], held[:done, :], preferred_element_type=jnp.float32)
        right[r, rows, :] = jnp.where(keep, solved, 0.0).astype(jnp.bfloat16)

    def row_of(dx, flip):
        return ((x + dx) % 4) * 2 + (1 - zh if flip else zh)

    def col_of(dy, flip, other=0):
        return ((y + dy) % 4) * 4 + (1 - zl if flip else zl) * 2 + (1 - h if other else h)

    sibling = col_of(0, 0, 1)

    def half(ref, slot, part):
        size = ref.shape[1] // CUTS
        return ref.at[slot, pl.ds(part * size, size), :]

    def send_right(slot, part, dx, flip=0):
        ref = half(right, slot, part)
        send(ref, ref, sem_right.at[slot, part], row_of(dx, flip), c, TO_ROW)

    def send_left(slot, part, dy, flip=0):
        ref = half(left, slot, part)
        send(ref, ref, sem_left.at[slot, part], r, col_of(dy, flip), TO_COL)

    def share(slot):
        send(left.at[slot], left.at[slot], sem_left.at[slot, 0], r, sibling, TO_COL)

    def wait_right(slot, part):
        arrived(half(right, slot, part), sem_right.at[slot, part])

    def wait_left(slot, part):
        arrived(half(left, slot, part), sem_left.at[slot, part])

    def wait_shared(slot):
        arrived(left.at[slot], sem_left.at[slot, 0])

    r_q, c_q = row_of(0, 1), col_of(0, 1)
    z_order = list(Z_ORDER)

    def along_z(count):
        for kind, part in z_order[:count]:
            if kind == RIGHT:
                send_right(r, part, 0, 1)
            else:
                send_left(c, part, 0, 1)
        del z_order[:count]

    for step in range(CUTS):
        for first, d in ((0, 1), (2, -1)):
            send_right(r, (first + step) % CUTS, d)
    for i in range(B // 256):
        rows = slice(i * 256, (i + 1) * 256)
        left[c, :, rows] = right[r, rows, :].astype(jnp.float32).T.astype(jnp.bfloat16)
    along_z(2)
    for step in range(CUTS):
        for first, d in ((0, 1), (2, -1)):
            send_left(c, (first + step) % CUTS, d)
        if step:
            along_z(2)
    share(c)
    cores_copy.wait()

    for step, *rest in STEPS:
        if step == NEAR:
            kind, flip, d, part = rest
            on = part // 2 == (0 if d == 1 else 1)
            if kind == RIGHT:
                wait_right(row_of(-d, flip), part)
                if on:
                    send_right(row_of(-d, flip), part, d)
            else:
                wait_left(col_of(-d, flip), part)
                if on and not (flip and part % 2):
                    send_left(col_of(-d, flip), part, d)
        elif step == FLIP:
            kind, part = rest
            if kind == RIGHT:
                wait_right(r_q, part)
            else:
                wait_left(c_q, part)
            for d in (1, -1):
                if kind == RIGHT:
                    send_right(r_q, part, d)
                else:
                    send_left(c_q, part, d)
        elif step == RELAY:
            wait_left(col_of(2, 0), rest[0])
            send_left(col_of(2, 0), rest[0], 0, 1)
        elif step == FAR:
            kind, flip = rest
            for part in range(CUTS):
                if kind == RIGHT:
                    wait_right(row_of(2, flip), part)
                elif flip or part % 2 == 0:
                    wait_left(col_of(2, flip), part)
        elif step == SHARE:
            share(col_of(*rest))
        elif step == WAIT:
            wait_shared(col_of(*rest, 1))
        else:
            dy, flip, pick = rest
            gram(left, right, out_ref, pair_at(y, zl, dy, flip), *rights_at(x, zh)[pick])

    assert sent[TO_ROW] % B == 0 and sent[TO_COL] % R == 0

    @pl.when(active)
    def _():
        left_device(moved.at[pl.ds(0, NP - 1)], sem_moved.at[0])
        left_device(spread.at[pl.ds(0, (PARTS - 1) * N_COL)], send_sem.at[SPREAD])

    @pl.when(jnp.logical_not(active))
    def _():
        left_device(spread.at[pl.ds(0, PARTS * N_COL)], send_sem.at[SPREAD])

    left_device(rank_rows.at[pl.ds(0, N_ROW - 1)], send_sem.at[RANK_A])
    left_device(rank_all.at[pl.ds(0, N_COL - 1)], send_sem.at[RANK_B])
    left_device(right.at[pl.ds(0, sent[TO_ROW] // B)], send_sem.at[TO_ROW])
    left_device(left.at[pl.ds(0, sent[TO_COL] // R)], send_sem.at[TO_COL])


def body(panel_right, factor_inverse, ranks, owner_map, cores):
    grams = 16 * 8 * 128 * 128
    vmem = pl.BlockSpec(memory_space=pltpu.VMEM)
    hbm = pl.BlockSpec(memory_space=pltpu.HBM)
    bf16 = jnp.bfloat16
    dma = pltpu.SemaphoreType.DMA
    out, right, left = pl.pallas_call(
        kernel,
        out_shape=(
            pltpu.VMEM((N_COL, N_ROW, R, R), jnp.float32),
            pltpu.VMEM((N_ROW, B, R), bf16),
            pltpu.VMEM((N_COL, R, B), bf16),
        ),
        in_specs=[hbm, hbm, hbm, hbm, hbm],
        out_specs=(vmem, vmem, vmem),
        scratch_shapes=[
            pltpu.SMEM((NP,), jnp.int32),
            pltpu.SMEM((1,), jnp.int32),
            pltpu.VMEM((N_COL, ROWS, R), bf16),
            pltpu.VMEM((NP, PART, R), bf16),
            pltpu.VMEM((NP, PART, R), bf16),
            pltpu.VMEM((B, R), bf16),
            pltpu.VMEM((B, B), bf16),
            pltpu.VMEM((8, R), jnp.int32),
            pltpu.VMEM((N_ROW, 8, R), jnp.int32),
            pltpu.VMEM((8, R), jnp.int32),
            pltpu.VMEM((N_COL, 8, R), jnp.int32),
            dma((5,)),
            dma((6,)),
            dma((N_ROW,)),
            dma((N_ROW,)),
            dma((N_COL,)),
            dma((1,)),
            dma((1,)),
            dma((N_ROW, CUTS)),
            dma((N_COL, CUTS)),
        ],
        compiler_params=pltpu.CompilerParams(
            collective_id=0, has_side_effects=True, vmem_limit_bytes=(46 << 20) + (512 << 10)),
        cost_estimate=pl.CostEstimate(
            flops=2 * grams * B, bytes_accessed=4 * grams * 2, transcendentals=0),
    )(owner_map, ranks, panel_right, factor_inverse, cores.reshape(N_COL, N_ROW, R, R))
    here = [pltpu.with_memory_space_constraint(v, pltpu.VMEM) for v in (left, right, out)]
    out, _ = pl.pallas_call(
        finish,
        out_shape=(jax.ShapeDtypeStruct(out.shape, jnp.float32), pltpu.VMEM(out.shape, jnp.float32)),
        in_specs=[vmem, vmem, vmem],
        out_specs=(hbm, vmem),
        input_output_aliases={2: 1},
        scratch_shapes=[dma((N_COL // 2,))],
        compiler_params=pltpu.CompilerParams(vmem_limit_bytes=8 << 20),
    )(*here)
    return out.reshape(cores.shape)


def solution(mesh):
    return jax.shard_map(
        body,
        mesh=mesh,
        in_specs=(
            P("row", "col", None),
            P(),
            P(("row", "col")),
            P(),
            P("row", "col", None, None, None, None),
        ),
        out_specs=P("row", "col", None, None, None, None),
        check_vma=False,
    )
```

```python
import jax
import jax.numpy as jnp
from jax import lax
from jax.experimental import pallas as pl
from jax.experimental.pallas import tpu as pltpu
from jax.sharding import PartitionSpec as P

B = 1536
R = 128
NP = 128
N_ROW = 8
N_COL = 16
ROWS = B // N_COL
PART = 16
PARTS = ROWS // PART
CUTS = 4
MESH = pl.DeviceIdType.MESH
NEAR, FAR, FLIP, RELAY, SHARE, WAIT, GRAM = range(7)
RIGHT, LEFT = 0, 1
Z_ORDER = (
    (LEFT, 0), (RIGHT, 0), (LEFT, 2), (RIGHT, 2), (LEFT, 1), (RIGHT, 1), (LEFT, 3), (RIGHT, 3),
)
STEPS = (
    (NEAR, RIGHT, 0, 1, 1), (FLIP, LEFT, 0), (FLIP, LEFT, 2), (NEAR, RIGHT, 0, -1, 2),
    (NEAR, LEFT, 0, -1, 3), (NEAR, LEFT, 0, 1, 0), (NEAR, LEFT, 0, -1, 2), (FLIP, RIGHT, 2),
    (FLIP, RIGHT, 0), (NEAR, LEFT, 0, 1, 1), (FLIP, LEFT, 1), (NEAR, LEFT, 0, -1, 0),
    (NEAR, RIGHT, 0, 1, 3), (NEAR, LEFT, 1, -1, 0), (FLIP, RIGHT, 1), (NEAR, LEFT, 0, 1, 2),
    (NEAR, RIGHT, 1, 1, 2), (NEAR, LEFT, 0, -1, 1), (FLIP, LEFT, 3), (NEAR, LEFT, 0, 1, 3),
    (NEAR, RIGHT, 0, -1, 1), (NEAR, RIGHT, 0, 1, 0), (NEAR, RIGHT, 0, -1, 3), (NEAR, LEFT, 1, 1, 0),
    (SHARE, 3, 0), (SHARE, 1, 0), (RELAY, 3), (SHARE, 0, 1),
    (FLIP, RIGHT, 3), (FAR, LEFT, 0), (RELAY, 1), (NEAR, LEFT, 1, -1, 2),
    (NEAR, RIGHT, 1, -1, 2), (SHARE, 2, 0), (WAIT, 0, 0), (NEAR, RIGHT, 0, 1, 2),
    (WAIT, 0, 1), (NEAR, RIGHT, 1, -1, 1), (NEAR, LEFT, 1, 1, 2), (FAR, RIGHT, 0),
    (NEAR, RIGHT, 0, -1, 0), (NEAR, RIGHT, 1, 1, 0), (WAIT, 1, 0), (NEAR, LEFT, 1, -1, 1),
    (NEAR, RIGHT, 1, -1, 0), (GRAM, 0, 1, 0), (NEAR, LEFT, 1, 1, 1), (WAIT, 3, 0),
    (GRAM, 1, 0, 0), (GRAM, 3, 0, 1), (WAIT, 2, 0), (GRAM, 0, 0, 0),
    (GRAM, 0, 0, 1), (NEAR, LEFT, 1, 1, 3), (GRAM, 2, 0, 0), (NEAR, LEFT, 1, -1, 3),
    (SHARE, 1, 1), (SHARE, 3, 1), (NEAR, RIGHT, 1, -1, 3), (NEAR, RIGHT, 1, 1, 3),
    (NEAR, RIGHT, 1, 1, 1), (GRAM, 1, 0, 1), (GRAM, 0, 1, 2), (GRAM, 0, 1, 1),
    (GRAM, 0, 0, 2), (GRAM, 2, 0, 2), (FAR, LEFT, 1),
    (GRAM, 3, 0, 0), (GRAM, 1, 0, 2), (GRAM, 2, 0, 1), (GRAM, 3, 0, 2),
    (WAIT, 3, 1), (WAIT, 1, 1), (GRAM, 1, 1, 1), (GRAM, 1, 1, 0),
    (GRAM, 3, 1, 1), (GRAM, 3, 1, 0), (GRAM, 1, 1, 2), (GRAM, 3, 1, 2),
    (FAR, RIGHT, 1), (WAIT, 2, 1),
)


def pair_at(y, zl, dy, flip):
    return ((y + dy) % 4) * 2 + (1 - zl if flip else zl)


def rights_at(x, zh):
    def row_of(dx, flip):
        return ((x + dx) % 4) * 2 + (1 - zh if flip else zh)

    return (
        (row_of(-1, 0), row_of(1, 0)),
        (row_of(0, 0), row_of(2, 0)),
        (row_of(-1, 1), row_of(1, 1)),
        (row_of(0, 1), row_of(2, 1)),
    )


def gram(left, right, out, pair, first, second):
    lhs = left[pl.ds(pair * 2, 2)].reshape(2 * R, B)
    rhs = jnp.concatenate([right[first], right[second]], axis=1)
    g = jnp.dot(lhs, rhs, preferred_element_type=jnp.float32)
    for i in range(2):
        for j, slot in enumerate((first, second)):
            out[pair * 2 + i, slot] -= g[i * R:(i + 1) * R, j * R:(j + 1) * R]


def finish(left, right, grams_in, out_hbm, grams, sem):
    r = lax.axis_index("row")
    c = lax.axis_index("col")
    x, zh, y, zl = r // 2, r % 2, c // 4, (c // 2) % 2
    done = {step[1:] for step in STEPS if step[0] == GRAM}
    copies = []
    for dy, flip in ((0, 0), (0, 1), (1, 0), (3, 0), (2, 0), (1, 1), (3, 1), (2, 1)):
        pair = pair_at(y, zl, dy, flip)
        for pick, rights in enumerate(rights_at(x, zh)):
            if (dy, flip, pick) not in done:
                gram(left, right, grams, pair, *rights)
        rows = pl.ds(pair * 2, 2)
        copy = pltpu.make_async_copy(grams.at[rows], out_hbm.at[rows], sem.at[len(copies)])
        copy.start()
        copies.append(copy)
    for copy in copies:
        copy.wait()


def kernel(owner_hbm, rank_hbm, panel_hbm, inverse_hbm, cores_hbm, out_ref, right, left,
           owner_ref, rank_ref, panel, spread, moved, held, inverse, rank_mine, rank_rows, rank_pack, rank_all,
           send_sem, local_sem, sem_spread, sem_rank_a, sem_rank_b, sem_moved, sem_rows,
           sem_right, sem_left):
    r = lax.axis_index("row")
    c = lax.axis_index("col")
    x, zh = r // 2, r % 2
    y, zl, h = c // 4, (c // 2) % 2, c % 2

    barrier = pltpu.get_barrier_semaphore()
    for d in range(1, N_ROW):
        pl.semaphore_signal(barrier, inc=1, device_id={"row": (r + d) % N_ROW, "col": c}, device_id_type=MESH)
    for d in range(1, N_COL):
        pl.semaphore_signal(barrier, inc=1, device_id={"row": r, "col": (c + d) % N_COL}, device_id_type=MESH)
    inverse_copy = pltpu.make_async_copy(inverse_hbm, inverse, local_sem.at[0])
    cores_copy = pltpu.make_async_copy(cores_hbm, out_ref, local_sem.at[1])
    panel_copy = pltpu.make_async_copy(panel_hbm, panel, local_sem.at[3])
    rank_copy = pltpu.make_async_copy(rank_hbm, rank_ref, local_sem.at[4])
    owner_copy = pltpu.make_async_copy(owner_hbm, owner_ref, local_sem.at[5])
    for copy in (panel_copy, rank_copy, owner_copy):
        copy.start()
    panel_copy.wait()
    pl.semaphore_wait(barrier, N_ROW + N_COL - 2)

    SPREAD, RANK_A, RANK_B, TO_ROW, TO_COL = range(5)
    sent = [0] * 5

    def send(src, dst, recv, row, col, group, when=None):
        desc = pltpu.make_async_remote_copy(
            src_ref=src, dst_ref=dst, send_sem=send_sem.at[group], recv_sem=recv,
            device_id={"row": row, "col": col}, device_id_type=MESH)
        sent[group] += src.shape[-3] if len(src.shape) == 3 else src.shape[-2]
        if when is None:
            desc.start()
        else:
            pl.when(when)(desc.start)

    def left_device(ref, sem):
        pltpu.make_async_remote_copy(
            src_ref=ref, dst_ref=ref, send_sem=sem, recv_sem=sem,
            device_id={"row": r, "col": c}, device_id_type=MESH).wait_send()

    def arrived(dst, recv):
        pltpu.make_async_remote_copy(
            src_ref=dst, dst_ref=dst, send_sem=recv, recv_sem=recv,
            device_id={"row": r, "col": c}, device_id_type=MESH).wait_recv()

    my_part = (r - c - 1) % N_ROW
    active = my_part < PARTS
    for d in range(1, N_ROW):
        to = (r + d) % N_ROW
        part = (to - c - 1) % N_ROW
        send(panel.at[:, pl.ds(pl.multiple_of(jnp.minimum(part, PARTS - 1) * PART, PART), PART), :],
             spread.at[pl.ds(r * N_COL, N_COL)], sem_spread.at[r], to, c, SPREAD, part < PARTS)
    own_part = pl.ds(pl.multiple_of(jnp.minimum(my_part, PARTS - 1) * PART, PART), PART)
    own_spread = pltpu.make_async_copy(
        panel.at[:, own_part, :], spread.at[pl.ds(r * N_COL, N_COL)], local_sem.at[2])
    pl.when(active)(own_spread.start)
    inverse_copy.start()

    rank_copy.wait()
    rank_mine[...] = jnp.full((8, R), rank_ref[0], jnp.int32)
    for d in range(1, N_ROW):
        send(rank_mine, rank_rows.at[r], sem_rank_a.at[r], (r + d) % N_ROW, c, RANK_A)
    rank_rows[r] = rank_mine[...]
    owner_copy.wait()

    @pl.when(active)
    def _():
        own_spread.wait()
        for d in range(1, N_ROW):
            frm = (r + d) % N_ROW
            arrived(spread.at[pl.ds(frm * N_COL, N_COL)], sem_spread.at[frm])

    me = r * N_COL + c
    own_rows = pl.ds(pl.multiple_of(c * ROWS + jnp.minimum(my_part, PARTS - 1) * PART, PART), PART)
    own_copy = pltpu.make_async_copy(moved.at[me], held.at[own_rows, :], local_sem.at[2])

    @pl.when(active)
    def _():
        @pl.loop(1, NP)
        def _(d):
            p = (r + d) % N_ROW * N_COL + (c + d // N_ROW) % N_COL
            moved[p] = spread[owner_ref[p]]
            pltpu.make_async_remote_copy(
                src_ref=moved.at[p], dst_ref=held.at[own_rows, :],
                send_sem=sem_moved.at[0], recv_sem=sem_rows.at[0],
                device_id={"row": p // N_COL, "col": p % N_COL}, device_id_type=MESH).start()
        moved[me] = spread[owner_ref[me]]
        own_copy.start()

    cores_copy.start()

    for d in range(1, N_ROW):
        frm = (r + d) % N_ROW
        arrived(rank_rows.at[frm], sem_rank_a.at[frm])
    for k in range(N_ROW):
        rank_pack[pl.ds(k, 1), :] = rank_rows[k, pl.ds(0, 1), :]
    for d in range(1, N_COL):
        send(rank_pack, rank_all.at[c], sem_rank_b.at[c], r, (c + d) % N_COL, RANK_B)
    rank_all[c] = rank_pack[...]
    for d in range(1, N_COL):
        frm = (c + d) % N_COL
        arrived(rank_all.at[frm], sem_rank_b.at[frm])
    inverse_copy.wait()

    @pl.when(active)
    def _():
        own_copy.wait()
        arrived(held.at[pl.ds(0, B - PART), :], sem_rows.at[0])

    @pl.when(jnp.logical_not(active))
    def _():
        arrived(held, sem_rows.at[0])

    block = owner_ref[r * N_COL + c]
    rank = rank_all[block % N_COL, pl.ds(block // N_COL, 1), :]
    keep = lax.broadcasted_iota(jnp.int32, (1, R), 1) < rank
    step = 256
    for i in range(B // step):
        rows = slice(i * step, (i + 1) * step)
        done = (i + 1) * step
        solved = jnp.dot(inverse[rows, :done], held[:done, :], preferred_element_type=jnp.float32)
        right[r, rows, :] = jnp.where(keep, solved, 0.0).astype(jnp.bfloat16)

    def row_of(dx, flip):
        return ((x + dx) % 4) * 2 + (1 - zh if flip else zh)

    def col_of(dy, flip, other=0):
        return ((y + dy) % 4) * 4 + (1 - zl if flip else zl) * 2 + (1 - h if other else h)

    sibling = col_of(0, 0, 1)

    def half(ref, slot, part):
        size = ref.shape[1] // CUTS
        return ref.at[slot, pl.ds(part * size, size), :]

    def send_right(slot, part, dx, flip=0):
        ref = half(right, slot, part)
        send(ref, ref, sem_right.at[slot, part], row_of(dx, flip), c, TO_ROW)

    def send_left(slot, part, dy, flip=0):
        ref = half(left, slot, part)
        send(ref, ref, sem_left.at[slot, part], r, col_of(dy, flip), TO_COL)

    def share(slot):
        send(left.at[slot], left.at[slot], sem_left.at[slot, 0], r, sibling, TO_COL)

    def wait_right(slot, part):
        arrived(half(right, slot, part), sem_right.at[slot, part])

    def wait_left(slot, part):
        arrived(half(left, slot, part), sem_left.at[slot, part])

    def wait_shared(slot):
        arrived(left.at[slot], sem_left.at[slot, 0])

    r_q, c_q = row_of(0, 1), col_of(0, 1)
    z_order = list(Z_ORDER)

    def along_z(count):
        for kind, part in z_order[:count]:
            if kind == RIGHT:
                send_right(r, part, 0, 1)
            else:
                send_left(c, part, 0, 1)
        del z_order[:count]

    for step in range(CUTS):
        for first, d in ((0, 1), (2, -1)):
            send_right(r, (first + step) % CUTS, d)
    for i in range(B // 256):
        rows = slice(i * 256, (i + 1) * 256)
        left[c, :, rows] = right[r, rows, :].astype(jnp.float32).T.astype(jnp.bfloat16)
    along_z(2)
    for step in range(CUTS):
        for first, d in ((0, 1), (2, -1)):
            send_left(c, (first + step) % CUTS, d)
        if step:
            along_z(2)
    share(c)
    cores_copy.wait()

    for step, *rest in STEPS:
        if step == NEAR:
            kind, flip, d, part = rest
            on = part // 2 == (0 if d == 1 else 1)
            if kind == RIGHT:
                wait_right(row_of(-d, flip), part)
                if on:
                    send_right(row_of(-d, flip), part, d)
            else:
                wait_left(col_of(-d, flip), part)
                if on and not (flip and part % 2):
                    send_left(col_of(-d, flip), part, d)
        elif step == FLIP:
            kind, part = rest
            if kind == RIGHT:
                wait_right(r_q, part)
            else:
                wait_left(c_q, part)
            for d in (1, -1):
                if kind == RIGHT:
                    send_right(r_q, part, d)
                else:
                    send_left(c_q, part, d)
        elif step == RELAY:
            wait_left(col_of(2, 0), rest[0])
            send_left(col_of(2, 0), rest[0], 0, 1)
        elif step == FAR:
            kind, flip = rest
            for part in (1, 3, 0, 2):
                if kind == RIGHT:
                    wait_right(row_of(2, flip), part)
                elif flip:
                    wait_left(col_of(2, 1), part)
                    ref = half(left, col_of(2, 1), part)
                    send(ref, ref, sem_left.at[col_of(2, 1), part], r, sibling, TO_COL)
                elif part % 2 == 0:
                    wait_left(col_of(2, 0), part)
        elif step == SHARE:
            share(col_of(*rest))
        elif step == WAIT and rest == [2, 1]:
            for part in range(CUTS):
                wait_left(col_of(2, 1, 1), part)
        elif step == WAIT:
            wait_shared(col_of(*rest, 1))
        else:
            dy, flip, pick = rest
            gram(left, right, out_ref, pair_at(y, zl, dy, flip), *rights_at(x, zh)[pick])

    assert sent[TO_ROW] % B == 0 and sent[TO_COL] % R == 0

    @pl.when(active)
    def _():
        left_device(moved.at[pl.ds(0, NP - 1)], sem_moved.at[0])
        left_device(spread.at[pl.ds(0, (PARTS - 1) * N_COL)], send_sem.at[SPREAD])

    @pl.when(jnp.logical_not(active))
    def _():
        left_device(spread.at[pl.ds(0, PARTS * N_COL)], send_sem.at[SPREAD])

    left_device(rank_rows.at[pl.ds(0, N_ROW - 1)], send_sem.at[RANK_A])
    left_device(rank_all.at[pl.ds(0, N_COL - 1)], send_sem.at[RANK_B])
    left_device(right.at[pl.ds(0, sent[TO_ROW] // B)], send_sem.at[TO_ROW])
    left_device(left.at[pl.ds(0, sent[TO_COL] // R)], send_sem.at[TO_COL])


def body(panel_right, factor_inverse, ranks, owner_map, cores):
    grams = 16 * 8 * 128 * 128
    vmem = pl.BlockSpec(memory_space=pltpu.VMEM)
    hbm = pl.BlockSpec(memory_space=pltpu.HBM)
    bf16 = jnp.bfloat16
    dma = pltpu.SemaphoreType.DMA
    out, right, left = pl.pallas_call(
        kernel,
        out_shape=(
            pltpu.VMEM((N_COL, N_ROW, R, R), jnp.float32),
            pltpu.VMEM((N_ROW, B, R), bf16),
            pltpu.VMEM((N_COL, R, B), bf16),
        ),
        in_specs=[hbm, hbm, hbm, hbm, hbm],
        out_specs=(vmem, vmem, vmem),
        scratch_shapes=[
            pltpu.SMEM((NP,), jnp.int32),
            pltpu.SMEM((1,), jnp.int32),
            pltpu.VMEM((N_COL, ROWS, R), bf16),
            pltpu.VMEM((NP, PART, R), bf16),
            pltpu.VMEM((NP, PART, R), bf16),
            pltpu.VMEM((B, R), bf16),
            pltpu.VMEM((B, B), bf16),
            pltpu.VMEM((8, R), jnp.int32),
            pltpu.VMEM((N_ROW, 8, R), jnp.int32),
            pltpu.VMEM((8, R), jnp.int32),
            pltpu.VMEM((N_COL, 8, R), jnp.int32),
            dma((5,)),
            dma((6,)),
            dma((N_ROW,)),
            dma((N_ROW,)),
            dma((N_COL,)),
            dma((1,)),
            dma((1,)),
            dma((N_ROW, CUTS)),
            dma((N_COL, CUTS)),
        ],
        compiler_params=pltpu.CompilerParams(
            collective_id=0, has_side_effects=True, vmem_limit_bytes=(46 << 20) + (512 << 10)),
        cost_estimate=pl.CostEstimate(
            flops=2 * grams * B, bytes_accessed=4 * grams * 2, transcendentals=0),
    )(owner_map, ranks, panel_right, factor_inverse, cores.reshape(N_COL, N_ROW, R, R))
    here = [pltpu.with_memory_space_constraint(v, pltpu.VMEM) for v in (left, right, out)]
    out, _ = pl.pallas_call(
        finish,
        out_shape=(jax.ShapeDtypeStruct(out.shape, jnp.float32), pltpu.VMEM(out.shape, jnp.float32)),
        in_specs=[vmem, vmem, vmem],
        out_specs=(hbm, vmem),
        input_output_aliases={2: 1},
        scratch_shapes=[dma((N_COL // 2,))],
        compiler_params=pltpu.CompilerParams(vmem_limit_bytes=8 << 20),
    )(*here)
    return out.reshape(cores.shape)


def solution(mesh):
    return jax.shard_map(
        body,
        mesh=mesh,
        in_specs=(
            P("row", "col", None),
            P(),
            P(("row", "col")),
            P(),
            P("row", "col", None, None, None, None),
        ),
        out_specs=P("row", "col", None, None, None, None),
        check_vma=False,
    )
```
